32 devices in a mesh: groups: 2 (over x), dp: 16 (over z, y, core).
Axes of the slice: x: 2, y: 2, z: 4, core: 2. Of those that a mesh axis runs over, the one named last changes fastest.
Arguments:
- layer_inputs: bfloat16 [4096, 2048], P(('groups', 'dp')), parts along dimension 0, may hold values from -0.125 to 0.125
- output_grads: bfloat16 [4096, 8192], P(('groups', 'dp')), parts along dimension 0, may hold values from -0.0625 to 0.0625
- query_grads: bfloat16 [128, 2, 512, 256], P('dp'), may hold values from -6 to 6
- eigenvalues: float32 [128, 512, 256], P('dp'), may hold values from 0.01 to 900, as said below
- out_basis: bfloat16 [64, 128, 128], replicated, may hold values from -0.5 to 0.5
- in_basis: bfloat16 [16, 128, 128], replicated, may hold values from -0.5 to 0.5
- doc_lengths: int32 [32], P('groups'), parts along dimension 0, may hold values from 1 to 512, 2048 in all
Outputs:
- influence: float32 [32, 2], P(('groups', 'dp')), parts along dimension 0
The draws below stay inside these ranges and needn't reach their ends.
There are 2 independent parts, one for each index of `groups`. The reference program is written for one: setup_inputs(seed, part) draws one part's arguments, and reference() takes and returns one part's arrays. A program takes and returns all parts, laid end to end along the dimension named above; an argument that names none is the same for every part. Nothing has to cross between parts.
Inputs may be any that keep to these rules, and one draw needn't show every extreme that they name: `doc_lengths`: the 16 lengths sum to 2048, and the largest is exactly 512. `eigenvalues`: positive.
All inputs are finite; a program needn't handle non-finite values.
Results may differ from the reference program's by a relative error of at most 0.0044.
Values may be sent and summed in bfloat16 or wider, within the bound.
A program may use at most 192 MiB of HBM per device.

```python
import math
import jax
import jax.numpy as jnp
import numpy as np
from jax import lax

DIN = 2048
DOUT = 8192
KB = 128
BO = 512
BI = 256
Q = 2
DOC_MAX = 512
NBLK = 128
TOKENS = 2048
DOCS = 16


def draw_eigenvalues(key, part):
    keys = jax.random.split(jax.random.fold_in(key, 17), 3)
    base = jnp.exp(jax.random.uniform(keys[0], (NBLK, BO, BI), jnp.float32, math.log(0.01), 0.0))
    top_factor = 3.0
    row_scale = jnp.exp(jax.random.uniform(keys[1], (NBLK, BO, 1), jnp.float32, 0.0, math.log(10.0)))
    col_scale = jnp.exp(jax.random.uniform(keys[2], (NBLK, 1, BI), jnp.float32, 0.0, math.log(10.0)))
    rising = 1.0 + (top_factor - 1.0) * jnp.arange(NBLK, dtype=jnp.float32)[:, None, None] / max(NBLK - 1, 1)
    return base * row_scale * col_scale * rising


def steps_of(rng, dims, cuts, low, high):
    level, own = 1.0, jax.random.fold_in(rng, 6)
    for dim, shards_of in cuts:
        draws = jnp.exp(jax.random.uniform(jax.random.fold_in(own, dim), (shards_of,), jnp.float32, low / len(cuts), high / len(cuts)))
        level = level * jnp.repeat(draws, dims[dim] // shards_of).reshape([-1 if axis == dim else 1 for axis in range(len(dims))])
    return level


def length_profile(number_of, total, most, slope):
    weights = [(1 << 20) // math.isqrt(rank ** slope) + 1 for rank in range(2, number_of + 1)]
    spare, given = total - most - (number_of - 1), [1] * (number_of - 1)
    while spare > 0:
        candidates = [i for i in range(number_of - 1) if given[i] < most]
        pool, budget = sum([weights[i] for i in candidates]), spare
        for i in candidates:
            addition = min(most - given[i], max(1, budget * weights[i] // pool), spare)
            given[i] = given[i] + addition
            spare = spare - addition
    return np.array([most] + given)


def ragged(stream_key, amount, total, limit, lean):
    if amount == 2:
        one = jax.random.randint(stream_key, (), max(1, total - limit), min(limit, total - 1) + 1)
        return jnp.stack([one, total - one])
    sizes = jnp.asarray(length_profile(amount, total, limit, lean), jnp.int32)
    couples = (amount - 1) // 2
    source_of, receiver = sizes[1:1 + 2 * couples:2], sizes[2:2 + 2 * couples:2]
    margin = jnp.minimum(source_of - 1, limit - receiver)
    moved = jax.random.randint(jax.random.fold_in(stream_key, 1), (couples,), 0, 1 << 20) % (margin + 1)
    sizes = sizes.at[1:1 + 2 * couples:2].set(source_of - moved).at[2:2 + 2 * couples:2].set(receiver + moved)
    return sizes[jax.random.permutation(jax.random.fold_in(stream_key, 2), amount)]


def normal_values(own_key, extent, deviation, bound, pieces=(), held_as=jnp.bfloat16):
    gain = steps_of(own_key, extent, pieces, -0.22, 0.18) if pieces else 1.0
    array = jax.random.normal(own_key, extent, jnp.float32) * deviation * gain
    return jnp.minimum(jnp.maximum(array, -bound), bound).astype(held_as)


def setup_inputs(seed: int = 0, part: int = 0) -> dict:
    splits = jax.random.split(jax.random.key(seed), 8)
    part_splits = jax.random.split(jax.random.fold_in(splits[7], part), 8)
    layer_inputs = normal_values(part_splits[0], (TOKENS, DIN), (DIN ** -0.5), 0.125, ((0, 16),))
    output_grads = normal_values(part_splits[1], (TOKENS, DOUT), (DOUT ** -0.5), 0.0625, ((0, 16),))
    query_grads = normal_values(splits[2], (NBLK, Q, BO, BI), 1.0, 6.0, ((0, 16),))
    eigenvalues = draw_eigenvalues(jax.random.fold_in(splits[7], 71), part)
    out_basis = normal_values(splits[4], (DOUT // KB, KB, KB), KB ** -0.5, 0.5)
    in_basis = normal_values(splits[5], (DIN // KB, KB, KB), KB ** -0.5, 0.5)
    doc_lengths = ragged(part_splits[6], DOCS, TOKENS, DOC_MAX, 2).astype(jnp.int32)
    return {"layer_inputs": layer_inputs, "output_grads": output_grads, "query_grads": query_grads, "eigenvalues": eigenvalues, "out_basis": out_basis, "in_basis": in_basis, "doc_lengths": doc_lengths}


def turn_rows(columns, basis_blocks):
    group_count = basis_blocks.shape[0]
    block_width = basis_blocks.shape[1]
    grouped = columns.reshape(columns.shape[0], group_count, block_width).astype(jnp.float32)
    turned = jnp.einsum('tnk,nkj->tnj', grouped, basis_blocks.astype(jnp.float32))
    return turned.reshape(columns.shape).astype(jnp.bfloat16)


def reference(layer_inputs, output_grads, query_grads, eigenvalues, out_basis, in_basis, doc_lengths):
    damping = 0.1 * jnp.mean(eigenvalues)
    rotated_grads = turn_rows(output_grads, out_basis)
    rotated_inputs = turn_rows(layer_inputs, in_basis)
    in_tiles = DIN // BI
    out_sets = out_basis.reshape(DOUT // BO, BO // KB, KB, KB)
    in_sets = in_basis.reshape(in_tiles, BI // KB, KB, KB)
    doc_ends = jnp.cumsum(doc_lengths).astype(jnp.int32)
    positions = jnp.arange(TOKENS, dtype=jnp.int32)
    doc_of = jnp.sum((positions[:, None] >= doc_ends[None, :]).astype(jnp.int32), axis=1).astype(jnp.int32)

    def one_tile(running, tile_index):
        out_id = (tile_index // in_tiles).astype(jnp.int32)
        in_id = (tile_index % in_tiles).astype(jnp.int32)
        grads = lax.dynamic_slice_in_dim(rotated_grads, (out_id * BO).astype(jnp.int32), BO, 1)
        inputs = lax.dynamic_slice_in_dim(rotated_inputs, (in_id * BI).astype(jnp.int32), BI, 1)
        tile_grads = lax.dynamic_index_in_dim(query_grads, tile_index, 0, keepdims=False)
        tile_eigen = lax.dynamic_index_in_dim(eigenvalues, tile_index, 0, keepdims=False)
        in_blocks = lax.dynamic_index_in_dim(in_sets, in_id, 0, keepdims=False)
        out_blocks = lax.dynamic_index_in_dim(out_sets, out_id, 0, keepdims=False)
        grouped = tile_grads.reshape(Q, BO, BI // KB, KB).astype(jnp.float32)
        half_turned = jnp.einsum('qonk,nkj->qonj', grouped, in_blocks.astype(jnp.float32))
        half_turned = half_turned.reshape(Q, BO, BI).astype(jnp.bfloat16)
        grouped = half_turned.reshape(Q, BO // KB, KB, BI).astype(jnp.float32)
        turned = jnp.einsum('qnki,nkj->qnji', grouped, out_blocks.astype(jnp.float32)).reshape(Q, BO, BI)
        preconditioned = (turned / (tile_eigen[None] + damping)).astype(jnp.bfloat16)
        projected = jnp.einsum('ti,qoi->tqo', inputs.astype(jnp.float32), preconditioned.astype(jnp.float32))
        return running + jnp.sum(projected * grads.astype(jnp.float32)[:, None, :], axis=2), None

    score, _ = lax.scan(one_tile, jnp.zeros((TOKENS, Q), jnp.float32), jnp.arange(NBLK, dtype=jnp.int32))
    return jax.ops.segment_sum(score, doc_of, num_segments=DOCS)
```

```python
import functools
import math

import jax
import jax.numpy as jnp
from jax import lax
from jax.experimental import pallas as pl
from jax.experimental.pallas import tpu as pltpu
from jax.sharding import PartitionSpec as P


def turn_rows(columns, basis_blocks):
    group_count = basis_blocks.shape[0]
    block_width = basis_blocks.shape[1]
    grouped = columns.reshape(columns.shape[0], group_count, block_width)
    turned = jnp.einsum("tnk,nkj->tnj", grouped, basis_blocks, preferred_element_type=jnp.float32)
    return turned.reshape(columns.shape).astype(jnp.bfloat16)


def precondition(query_grads, eigenvalues, damping, tile_out, tile_in):
    blocks, queries, rows_out, rows_in = query_grads.shape
    block_width = tile_in.shape[-1]
    grouped = query_grads.reshape(blocks, queries, rows_out, rows_in // block_width, block_width)
    half_turned = jnp.einsum(
        "bqonk,bnkj->bqonj", grouped, tile_in, preferred_element_type=jnp.float32
    )
    half_turned = half_turned.reshape(blocks, queries, rows_out, rows_in).astype(jnp.bfloat16)
    grouped = half_turned.reshape(blocks, queries, rows_out // block_width, block_width, rows_in)
    turned = jnp.einsum("bqnki,bnkj->bqnji", grouped, tile_out, preferred_element_type=jnp.float32)
    turned = turned.reshape(blocks, queries, rows_out, rows_in)
    return (turned / (eigenvalues[:, None] + damping)).astype(jnp.bfloat16)


def tally_scores(grads_got, inputs_got, preconditioned, doc_starts, doc_ends):
    blocks, total_rows, rows_out = grads_got.shape
    queries = preconditioned.shape[1]
    row_step = math.gcd(1024, total_rows)
    flat_pre = preconditioned.reshape(blocks, queries * rows_out, preconditioned.shape[3])

    def one_piece(running, piece_index):
        start_row = piece_index * row_step
        grads_piece = lax.dynamic_slice_in_dim(grads_got, start_row, row_step, 1)
        inputs_piece = lax.dynamic_slice_in_dim(inputs_got, start_row, row_step, 1)
        projected = jnp.einsum(
            "bti,bpi->btp", inputs_piece, flat_pre, preferred_element_type=jnp.float32
        )
        projected = projected.reshape(blocks, row_step, queries, rows_out)
        scores = jnp.sum(projected * grads_piece[:, :, None, :].astype(jnp.float32), axis=(0, 3))
        positions = start_row + lax.iota(jnp.int32, row_step)
        member = (
            (positions[:, None] >= doc_starts[None, :]) & (positions[:, None] < doc_ends[None, :])
        ).astype(jnp.float32)
        added = jnp.einsum("td,tq->dq", member, scores, precision=lax.Precision.HIGHEST)
        return (running + added, None)

    initial = jnp.zeros((doc_starts.shape[0], queries), jnp.float32)
    summed, _ = lax.scan(one_piece, initial, jnp.arange(total_rows // row_step, dtype=jnp.int32))
    return summed


def tiles_apart(layer_inputs, output_grads, query_grads, eigenvalues, out_basis, in_basis, doc_lengths):
    block_width = out_basis.shape[1]
    tok_count = layer_inputs.shape[0]
    tile_count = query_grads.shape[0]
    rows_out = query_grads.shape[2]
    rows_in = query_grads.shape[3]
    in_tiles = layer_inputs.shape[1] // rows_in
    out_tiles = output_grads.shape[1] // rows_out
    tile_ids = lax.axis_index("dp") * tile_count + lax.iota(jnp.int32, tile_count)
    out_sets = out_basis.reshape(out_tiles, rows_out // block_width, block_width, block_width)
    in_sets = in_basis.reshape(in_tiles, rows_in // block_width, block_width, block_width)
    tile_out = jnp.take(out_sets, tile_ids // in_tiles, axis=0)
    tile_in = jnp.take(in_sets, tile_ids % in_tiles, axis=0)
    eigen_sum = lax.psum(jnp.sum(eigenvalues), "dp")
    entries = output_grads.shape[1] * layer_inputs.shape[1]
    damping = 0.1 * (eigen_sum / entries)
    preconditioned = precondition(query_grads, eigenvalues, damping, tile_out, tile_in)
    grads_local = turn_rows(output_grads, out_basis)
    inputs_local = turn_rows(layer_inputs, in_basis)
    grads_tiles = grads_local.reshape(tok_count, out_tiles, rows_out).transpose(1, 0, 2)[:, None]
    grads_tiles = jnp.broadcast_to(grads_tiles, (out_tiles, in_tiles, tok_count, rows_out))
    grads_tiles = grads_tiles.reshape(out_tiles * in_tiles, tok_count, rows_out)
    inputs_tiles = inputs_local.reshape(tok_count, in_tiles, rows_in).transpose(1, 0, 2)[None]
    inputs_tiles = jnp.broadcast_to(inputs_tiles, (out_tiles, in_tiles, tok_count, rows_in))
    inputs_tiles = inputs_tiles.reshape(out_tiles * in_tiles, tok_count, rows_in)
    grads_got, inputs_got = (
        lax.all_to_all(grads_tiles, "dp", split_axis=0, concat_axis=1, tiled=True),
        lax.all_to_all(inputs_tiles, "dp", split_axis=0, concat_axis=1, tiled=True),
    )
    doc_ends = jnp.cumsum(doc_lengths)
    doc_starts = doc_ends - doc_lengths
    partial_scores = tally_scores(grads_got, inputs_got, preconditioned, doc_starts, doc_ends)
    return lax.psum_scatter(partial_scores, "dp", scatter_dimension=0, tiled=True)


CORES = 2
ROWS = 2
PARTS = 2
LANES = 128
MESH = pl.DeviceIdType.MESH


def fused_kernel(
    n, eigen_count,
    x_ref, y_ref, query_ref, eigen_ref, outb_ref, inb_ref, lengths_ref,
    out_ref,
    x_all, y_all, query, eigen, outb, inb, outb_t, pre, rotated, grads_rot, projected, lengths, e_buf, f_buf, acc,
    local_sem, x_send, x_recv, y_send, y_recv, e_send, e_recv, f_send, f_recv, plane_in, below_in, above_in,
):
    planes = n // (CORES * ROWS)
    group, me = lax.axis_index("groups"), lax.axis_index("dp")
    core = lax.rem(me, CORES)
    row = lax.rem(me // CORES, ROWS)
    plane = me // (CORES * ROWS)
    tokens, width_in = x_ref.shape
    width_out = y_all.shape[2]
    tiles, queries, rows_out, rows_in = query_ref.shape
    block = outb_ref.shape[1]
    out_blocks = rows_out // block
    in_blocks = width_in // block
    blocks_per_tile = rows_in // block

    def slot_of(p, r, c):
        return (p * ROWS + r) * CORES + c

    up, down = me + CORES * ROWS, me - CORES * ROWS
    across = slot_of(plane, 1 - row, core)
    partner = slot_of(plane, row, 1 - core)
    has_up, has_down = plane < planes - 1, plane > 0
    at_end = (plane == 0) | (plane == planes - 1)

    def x_copy(src, slot, channel, target, part):
        span = pl.ds(part * (tokens // PARTS), tokens // PARTS)
        return pltpu.make_async_remote_copy(
            src_ref=src.at[span], dst_ref=x_all.at[slot, span],
            send_sem=x_send.at[slot * PARTS + part, channel],
            recv_sem=x_recv.at[slot * PARTS + part],
            device_id=(group, target), device_id_type=MESH,
        )

    def x_arrived(slot, part):
        x_copy(x_all.at[slot], slot, 0, across, part).wait_recv()

    def x_forward(slot, channel, target, part):
        x_copy(x_all.at[slot], slot, channel, target, part).start()

    def y_copy(target):
        columns = pl.ds(pl.multiple_of(target * width_out, width_out), width_out)
        return pltpu.make_async_remote_copy(
            src_ref=y_ref.at[:, columns], dst_ref=y_all.at[me],
            send_sem=y_send.at[target], recv_sem=y_recv.at[me],
            device_id=(group, target), device_id_type=MESH,
        )

    def y_arrived(source):
        pltpu.make_async_remote_copy(
            src_ref=y_all.at[source], dst_ref=y_all.at[source],
            send_sem=y_send.at[source], recv_sem=y_recv.at[source],
            device_id=(group, across), device_id_type=MESH,
        ).wait_recv()

    def small_copy(buf, send, recv, source, target):
        return pltpu.make_async_remote_copy(
            src_ref=buf.at[source], dst_ref=buf.at[source],
            send_sem=send.at[target], recv_sem=recv.at[source],
            device_id=(group, target), device_id_type=MESH,
        )

    def loop(low, high, body):
        def step(j, carry):
            body(j)
            return carry
        lax.fori_loop(low, high, step, 0)

    def others(body):
        loop(1, n, lambda j: body(lax.rem(me + j, n)))

    def y_send_plane(p):
        loop(0, ROWS * CORES, lambda j: y_copy(slot_of(p, 0, 0) + lax.rem(me + j, ROWS * CORES)).start())

    def sides(k, body):
        def one(side):
            p = plane + k * (2 * side - 1)
            @pl.when((p >= 0) & (p < planes))
            def _():
                body(p)
        loop(0, 2, one)

    def from_across(p):
        slot = slot_of(p, 1 - row, core)
        for part in range(PARTS):
            x_arrived(slot, part)
            x_forward(slot, 3, partner, part)

    def from_line(p):
        slot = slot_of(p, row, core)
        for part in range(PARTS):
            x_arrived(slot, part)

            @pl.when((p < plane) & has_up)
            def _():
                x_forward(slot, 0, up, part)

            @pl.when((p > plane) & has_down)
            def _():
                x_forward(slot, 1, down, part)

            x_forward(slot, 2, across, part)
            x_forward(slot, 3, partner, part)

    def lines(k):
        sides(k, from_line)

        @pl.when((plane == k) & has_up)
        def _():
            loop(0, planes - 1 - plane, lambda j: y_send_plane(planes - 1 - j))

        @pl.when((planes - 1 - plane == k) & has_down)
        def _():
            loop(0, plane, y_send_plane)

    own_columns = pl.ds(pl.multiple_of(me * width_out, width_out), width_out)
    own_out = pl.ds(me * out_blocks, out_blocks)
    loads = [
        pltpu.make_async_copy(eigen_ref, eigen, local_sem.at[0]),
        pltpu.make_async_copy(query_ref, query, local_sem.at[1]),
        pltpu.make_async_copy(outb_ref.at[own_out], outb, local_sem.at[2]),
        pltpu.make_async_copy(inb_ref, inb, local_sem.at[3]),
        pltpu.make_async_copy(x_ref, x_all.at[me], local_sem.at[4]),
        pltpu.make_async_copy(y_ref.at[:, own_columns], y_all.at[me], local_sem.at[5]),
    ]

    barrier = pltpu.get_barrier_semaphore()

    def greet(semaphore, target):
        pl.semaphore_signal(semaphore, inc=1, device_id=(group, target), device_id_type=MESH)

    @pl.when(has_up)
    def _():
        greet(barrier, up)

    @pl.when(has_down)
    def _():
        greet(barrier, down)

    greet(barrier, across)
    greet(barrier, partner)
    for load in loads:
        load.start()
    pl.semaphore_wait(barrier, 2 + has_up.astype(jnp.int32) + has_down.astype(jnp.int32))

    for part in range(PARTS):
        @pl.when(has_up)
        def _():
            x_copy(x_ref, me, 0, up, part).start()

        @pl.when(has_down)
        def _():
            x_copy(x_ref, me, 1, down, part).start()

        x_copy(x_ref, me, 2, across, part).start()
        x_copy(x_ref, me, 3, partner, part).start()

    greet(plane_in, partner)
    y_copy(partner).start()
    pl.semaphore_wait(plane_in, 1)

    @pl.when(plane == 0)
    def _():
        greet(below_in, up)

    @pl.when(plane == planes - 1)
    def _():
        greet(above_in, down)

    loads[0].wait()

    def add_tile(b, carry):
        tile = eigen[b]
        folded = tile[:, :LANES]
        for lane in range(LANES, rows_in, LANES):
            folded = folded + tile[:, lane:lane + LANES]
        return carry + jnp.sum(folded.reshape(rows_out // 8, 8, LANES), axis=0)

    e_buf[me] = lax.fori_loop(0, tiles, add_tile, jnp.zeros((8, LANES), jnp.float32))

    @pl.when(has_down)
    def _():
        pl.semaphore_wait(below_in, 1)

        @pl.when(has_up)
        def _():
            greet(below_in, up)

    @pl.when(has_up)
    def _():
        pl.semaphore_wait(above_in, 1)

        @pl.when(has_down)
        def _():
            greet(above_in, down)

    others(lambda t: small_copy(e_buf, e_send, e_recv, me, t).start())

    @pl.when(at_end)
    def _():
        def outward(j):
            k = jnp.where(j == 0, 1, planes - j)
            y_send_plane(jnp.where(plane == 0, k, planes - 1 - k))
        loop(0, planes - 1, outward)

    for load in loads[1:4]:
        load.wait()
    for j in range(out_blocks):
        outb_t[j] = outb[j].astype(jnp.float32).T.astype(jnp.bfloat16)

    def half_turn(b):
        for q in range(queries):
            for k in range(blocks_per_tile):
                lanes = slice(k * block, (k + 1) * block)
                query[b, q, :, lanes] = jnp.dot(
                    query[b, q, :, lanes], inb[b * blocks_per_tile + k],
                    preferred_element_type=jnp.float32,
                ).astype(jnp.bfloat16)

    loop(0, tiles, half_turn)
    lines(1)
    others(lambda t: small_copy(e_buf, e_send, e_recv, t, t).wait_recv())
    damping = 0.1 * (jnp.sum(e_buf[...]) / eigen_count)

    def finish(b):
        columns = pl.ds(pl.multiple_of(b * rows_in, rows_in), rows_in)
        for j in range(out_blocks):
            span = slice(j * block, (j + 1) * block)
            inverse = 1.0 / (eigen[b, span, :] + damping)
            for q in range(queries):
                turned = jnp.dot(outb_t[j], query[b, q, span, :], preferred_element_type=jnp.float32)
                pre[q * rows_out + j * block:q * rows_out + (j + 1) * block, columns] = (
                    turned * inverse
                ).astype(jnp.bfloat16)

    loop(0, tiles, finish)
    for load in loads[4:]:
        load.wait()
    acc[...] = jnp.zeros_like(acc)
    lanes_of_docs = acc.shape[1]
    rows = CORES * tokens
    docs = lengths_ref.shape[1]
    lengths[...] = jnp.zeros_like(lengths)
    lengths[0:1, 0:docs] = lengths_ref[...].astype(jnp.float32)
    lengths_row = lengths[0:1, :]
    lengths_down = jnp.broadcast_to(lengths_row, (lanes_of_docs, lanes_of_docs)).T
    earlier = lax.broadcasted_iota(jnp.int32, lengths_down.shape, 0)
    earlier = earlier <= lax.broadcasted_iota(jnp.int32, lengths_down.shape, 1)
    ends = jnp.sum(jnp.where(earlier, lengths_down, 0.0), axis=0, keepdims=True)
    lengths[1:2, :] = ends
    lengths[0:1, :] = ends - lengths_row

    def project_chip(p, r):
        base = slot_of(p, r, 0)
        for part in range(PARTS):
            x_arrived(base + 1 - core, part)
        for c in range(CORES):
            spot = slice(c * tokens, (c + 1) * tokens)
            for k in range(in_blocks):
                lanes = slice(k * block, (k + 1) * block)
                rotated[spot, lanes] = jnp.dot(
                    x_all[base + c, :, lanes], inb[k], preferred_element_type=jnp.float32
                ).astype(jnp.bfloat16)
        step = math.gcd(queries * rows_out, 256)
        for o in range(0, queries * rows_out, step):
            projected[p * ROWS + r, :, o:o + step] = lax.dot_general(
                rotated[...], pre[o:o + step, :], (((1,), (1,)), ((), ())),
                preferred_element_type=jnp.float32,
            )

    def tally_chip(p, r):
        base = slot_of(p, r, 0)
        for c in range(CORES):
            @pl.when(base + c != me)
            def _():
                y_arrived(base + c)
        for c in range(CORES):
            spot = slice(c * tokens, (c + 1) * tokens)
            for k in range(out_blocks):
                lanes = slice(k * block, (k + 1) * block)
                grads_rot[spot, lanes] = jnp.dot(
                    y_all[base + c, :, lanes], outb[k], preferred_element_type=jnp.float32
                ).astype(jnp.bfloat16).astype(jnp.float32)
        positions = base * tokens + lax.broadcasted_iota(jnp.int32, (rows, lanes_of_docs), 0)
        positions = positions.astype(jnp.float32)
        member = (positions >= lengths[0:1, :]) & (positions < lengths[1:2, :])
        for q in range(queries):
            total = jnp.zeros((rows, LANES), jnp.float32)
            for lane in range(0, rows_out, LANES):
                total = total + (
                    projected[p * ROWS + r, :, q * rows_out + lane:q * rows_out + lane + LANES]
                    * grads_rot[:, lane:lane + LANES]
                )
            score = jnp.sum(total, axis=1, keepdims=True)
            added = jnp.sum(jnp.where(member, score, 0.0), axis=0, keepdims=True)
            acc[q:q + 1, :] = acc[q:q + 1, :] + added

    def project_plane(p):
        from_across(p)
        loop(0, ROWS, lambda r: project_chip(p, lax.rem(row + r, ROWS)))

    project_plane(plane)
    loop(2, planes, lines)

    y_copy(across).start()
    y_copy(slot_of(plane, 1 - row, 1 - core)).start()
    loop(1, planes, lambda k: sides(k, project_plane))
    turn = jnp.where(2 * plane < planes, planes - 1, 1)

    def tally_plane(j):
        p = lax.rem(plane + turn * j, planes)
        loop(0, ROWS, lambda r: tally_chip(p, lax.rem(row + r, ROWS)))

    loop(0, planes, tally_plane)
    f_buf[me] = acc[...]
    others(lambda t: small_copy(f_buf, f_send, f_recv, me, t).start())

    def left(slot, channel):
        for part in range(PARTS):
            x_copy(x_all.at[slot], slot, channel, across, part).wait_send()

    def drain(p):
        slot = slot_of(p, row, core)

        @pl.when((p <= plane) & has_up)
        def _():
            left(slot, 0)

        @pl.when((p >= plane) & has_down)
        def _():
            left(slot, 1)

        left(slot, 2)
        left(slot, 3)
        left(slot_of(p, 1 - row, core), 3)

    loop(0, planes, drain)
    others(lambda t: y_copy(t).wait_send())
    others(lambda t: small_copy(e_buf, e_send, e_recv, me, t).wait_send())
    others(lambda t: small_copy(f_buf, f_send, f_recv, t, t).wait_recv())
    others(lambda t: small_copy(f_buf, f_send, f_recv, me, t).wait_send())
    summed = jnp.sum(f_buf[...], axis=0)
    lane = lax.broadcasted_iota(jnp.int32, summed.shape, 1)
    per_device = out_ref.shape[0]
    for j in range(per_device):
        picked = jnp.sum(jnp.where(lane == me * per_device + j, summed, 0.0), axis=1, keepdims=True)
        for q in range(queries):
            out_ref[j:j + 1, q:q + 1] = picked[q:q + 1, :]


def fused(n, layer_inputs, output_grads, query_grads, eigenvalues, out_basis, in_basis, doc_lengths):
    tokens, width_in = layer_inputs.shape
    tiles, queries, rows_out, rows_in = query_grads.shape
    docs = doc_lengths.shape[0]
    block = out_basis.shape[1]
    anyspace = pl.BlockSpec(memory_space=pl.ANY)
    vmem = pl.BlockSpec(memory_space=pltpu.VMEM)
    bf16, f32 = jnp.bfloat16, jnp.float32
    return pl.pallas_call(
        functools.partial(fused_kernel, n, output_grads.shape[1] * width_in),
        out_shape=jax.ShapeDtypeStruct((docs // n, queries), f32),
        in_specs=[anyspace] * 6 + [vmem],
        out_specs=vmem,
        scratch_shapes=[
            pltpu.VMEM((n, tokens, width_in), bf16),
            pltpu.VMEM((n, tokens, rows_out), bf16),
            pltpu.VMEM(query_grads.shape, bf16),
            pltpu.VMEM(eigenvalues.shape, f32),
            pltpu.VMEM((rows_out // block, block, block), bf16),
            pltpu.VMEM(in_basis.shape, bf16),
            pltpu.VMEM((rows_out // block, block, block), bf16),
            pltpu.VMEM((queries * rows_out, width_in), bf16),
            pltpu.VMEM((CORES * tokens, width_in), bf16),
            pltpu.VMEM((CORES * tokens, rows_out), f32),
            pltpu.VMEM((n // CORES, CORES * tokens, queries * rows_out), f32),
            pltpu.VMEM((8, LANES), f32),
            pltpu.VMEM((n, 8, LANES), f32),
            pltpu.VMEM((n, 8, LANES), f32),
            pltpu.VMEM((8, LANES), f32),
            pltpu.SemaphoreType.DMA((6,)),
            pltpu.SemaphoreType.DMA((n * PARTS, 4)),
            pltpu.SemaphoreType.DMA((n * PARTS,)),
        ] + [pltpu.SemaphoreType.DMA((n,))] * 6 + [pltpu.SemaphoreType.REGULAR] * 3,
        compiler_params=pltpu.CompilerParams(
            collective_id=0, has_side_effects=True, vmem_limit_bytes=60 * 1024 * 1024
        ),
    )(layer_inputs, output_grads, query_grads, eigenvalues, out_basis, in_basis, doc_lengths[None])


def local(n, *arrays):
    layer_inputs, output_grads, query_grads, _, _, _, doc_lengths = arrays
    tiles, queries, rows_out, rows_in = query_grads.shape
    whole_rows = tiles * rows_in == layer_inputs.shape[1] and n * rows_out == output_grads.shape[1]
    fits = n * layer_inputs.size <= 8 * query_grads.size and doc_lengths.shape[0] <= LANES
    shaped = n % (CORES * ROWS) == 0 and doc_lengths.shape[0] % n == 0 and queries <= 8
    shaped = shaped and layer_inputs.shape[0] % (16 * PARTS) == 0 and n > CORES * ROWS
    if whole_rows and fits and shaped:
        return fused(n, *arrays)
    return tiles_apart(*arrays)


def solution(mesh):
    in_specs = (
        P(("groups", "dp"), None),
        P(("groups", "dp"), None),
        P("dp", None, None, None),
        P("dp", None, None),
        P(),
        P(),
        P("groups"),
    )
    out_specs = P(("groups", "dp"), None)
    return jax.shard_map(functools.partial(local, mesh.shape["dp"]), mesh=mesh, in_specs=in_specs, out_specs=out_specs, check_vma=False)
```

```python
import functools
import math

import jax
import jax.numpy as jnp
from jax import lax
from jax.experimental import pallas as pl
from jax.experimental.pallas import tpu as pltpu
from jax.sharding import PartitionSpec as P


def turn_rows(columns, basis_blocks):
    group_count = basis_blocks.shape[0]
    block_width = basis_blocks.shape[1]
    grouped = columns.reshape(columns.shape[0], group_count, block_width)
    turned = jnp.einsum("tnk,nkj->tnj", grouped, basis_blocks, preferred_element_type=jnp.float32)
    return turned.reshape(columns.shape).astype(jnp.bfloat16)


def precondition(query_grads, eigenvalues, damping, tile_out, tile_in):
    blocks, queries, rows_out, rows_in = query_grads.shape
    block_width = tile_in.shape[-1]
    grouped = query_grads.reshape(blocks, queries, rows_out, rows_in // block_width, block_width)
    half_turned = jnp.einsum(
        "bqonk,bnkj->bqonj", grouped, tile_in, preferred_element_type=jnp.float32
    )
    half_turned = half_turned.reshape(blocks, queries, rows_out, rows_in).astype(jnp.bfloat16)
    grouped = half_turned.reshape(blocks, queries, rows_out // block_width, block_width, rows_in)
    turned = jnp.einsum("bqnki,bnkj->bqnji", grouped, tile_out, preferred_element_type=jnp.float32)
    turned = turned.reshape(blocks, queries, rows_out, rows_in)
    return (turned / (eigenvalues[:, None] + damping)).astype(jnp.bfloat16)


def tally_scores(grads_got, inputs_got, preconditioned, doc_starts, doc_ends):
    blocks, total_rows, rows_out = grads_got.shape
    queries = preconditioned.shape[1]
    row_step = math.gcd(1024, total_rows)
    flat_pre = preconditioned.reshape(blocks, queries * rows_out, preconditioned.shape[3])

    def one_piece(running, piece_index):
        start_row = piece_index * row_step
        grads_piece = lax.dynamic_slice_in_dim(grads_got, start_row, row_step, 1)
        inputs_piece = lax.dynamic_slice_in_dim(inputs_got, start_row, row_step, 1)
        projected = jnp.einsum(
            "bti,bpi->btp", inputs_piece, flat_pre, preferred_element_type=jnp.float32
        )
        projected = projected.reshape(blocks, row_step, queries, rows_out)
        scores = jnp.sum(projected * grads_piece[:, :, None, :].astype(jnp.float32), axis=(0, 3))
        positions = start_row + lax.iota(jnp.int32, row_step)
        member = (
            (positions[:, None] >= doc_starts[None, :]) & (positions[:, None] < doc_ends[None, :])
        ).astype(jnp.float32)
        added = jnp.einsum("td,tq->dq", member, scores, precision=lax.Precision.HIGHEST)
        return (running + added, None)

    initial = jnp.zeros((doc_starts.shape[0], queries), jnp.float32)
    summed, _ = lax.scan(one_piece, initial, jnp.arange(total_rows // row_step, dtype=jnp.int32))
    return summed


def tiles_apart(layer_inputs, output_grads, query_grads, eigenvalues, out_basis, in_basis, doc_lengths):
    block_width = out_basis.shape[1]
    tok_count = layer_inputs.shape[0]
    tile_count = query_grads.shape[0]
    rows_out = query_grads.shape[2]
    rows_in = query_grads.shape[3]
    in_tiles = layer_inputs.shape[1] // rows_in
    out_tiles = output_grads.shape[1] // rows_out
    tile_ids = lax.axis_index("dp") * tile_count + lax.iota(jnp.int32, tile_count)
    out_sets = out_basis.reshape(out_tiles, rows_out // block_width, block_width, block_width)
    in_sets = in_basis.reshape(in_tiles, rows_in // block_width, block_width, block_width)
    tile_out = jnp.take(out_sets, tile_ids // in_tiles, axis=0)
    tile_in = jnp.take(in_sets, tile_ids % in_tiles, axis=0)
    eigen_sum = lax.psum(jnp.sum(eigenvalues), "dp")
    entries = output_grads.shape[1] * layer_inputs.shape[1]
    damping = 0.1 * (eigen_sum / entries)
    preconditioned = precondition(query_grads, eigenvalues, damping, tile_out, tile_in)
    grads_local = turn_rows(output_grads, out_basis)
    inputs_local = turn_rows(layer_inputs, in_basis)
    grads_tiles = grads_local.reshape(tok_count, out_tiles, rows_out).transpose(1, 0, 2)[:, None]
    grads_tiles = jnp.broadcast_to(grads_tiles, (out_tiles, in_tiles, tok_count, rows_out))
    grads_tiles = grads_tiles.reshape(out_tiles * in_tiles, tok_count, rows_out)
    inputs_tiles = inputs_local.reshape(tok_count, in_tiles, rows_in).transpose(1, 0, 2)[None]
    inputs_tiles = jnp.broadcast_to(inputs_tiles, (out_tiles, in_tiles, tok_count, rows_in))
    inputs_tiles = inputs_tiles.reshape(out_tiles * in_tiles, tok_count, rows_in)
    grads_got, inputs_got = (
        lax.all_to_all(grads_tiles, "dp", split_axis=0, concat_axis=1, tiled=True),
        lax.all_to_all(inputs_tiles, "dp", split_axis=0, concat_axis=1, tiled=True),
    )
    doc_ends = jnp.cumsum(doc_lengths)
    doc_starts = doc_ends - doc_lengths
    partial_scores = tally_scores(grads_got, inputs_got, preconditioned, doc_starts, doc_ends)
    return lax.psum_scatter(partial_scores, "dp", scatter_dimension=0, tiled=True)


CORES = 2
ROWS = 2
PARTS = 2
LANES = 128
MESH = pl.DeviceIdType.MESH


def fused_kernel(
    n, eigen_count,
    x_ref, y_ref, query_ref, eigen_ref, outb_ref, inb_ref, lengths_ref,
    out_ref,
    x_all, y_all, query, eigen, outb, inb, outb_t, pre, rotated, grads_rot, projected, lengths, e_buf, f_buf, acc,
    local_sem, x_send, x_recv, y_send, y_recv, e_send, e_recv, f_send, f_recv, plane_in, below_in, above_in,
):
    planes = n // (CORES * ROWS)
    group, me = lax.axis_index("groups"), lax.axis_index("dp")
    core = lax.rem(me, CORES)
    row = lax.rem(me // CORES, ROWS)
    plane = me // (CORES * ROWS)
    tokens, width_in = x_ref.shape
    width_out = y_all.shape[2]
    tiles, queries, rows_out, rows_in = query_ref.shape
    block = outb_ref.shape[1]
    out_blocks = rows_out // block
    in_blocks = width_in // block
    blocks_per_tile = rows_in // block

    def slot_of(p, r, c):
        return (p * ROWS + r) * CORES + c

    up, down = me + CORES * ROWS, me - CORES * ROWS
    across = slot_of(plane, 1 - row, core)
    partner = slot_of(plane, row, 1 - core)
    has_up, has_down = plane < planes - 1, plane > 0
    at_end = (plane == 0) | (plane == planes - 1)

    def x_copy(src, slot, channel, target, part):
        span = pl.ds(part * (tokens // PARTS), tokens // PARTS)
        return pltpu.make_async_remote_copy(
            src_ref=src.at[span], dst_ref=x_all.at[slot, span],
            send_sem=x_send.at[slot * PARTS + part, channel],
            recv_sem=x_recv.at[slot * PARTS + part],
            device_id=(group, target), device_id_type=MESH,
        )

    def x_arrived(slot, part):
        x_copy(x_all.at[slot], slot, 0, across, part).wait_recv()

    def x_forward(slot, channel, target, part):
        x_copy(x_all.at[slot], slot, channel, target, part).start()

    def y_copy(target):
        columns = pl.ds(pl.multiple_of(target * width_out, width_out), width_out)
        return pltpu.make_async_remote_copy(
            src_ref=y_ref.at[:, columns], dst_ref=y_all.at[me],
            send_sem=y_send.at[target], recv_sem=y_recv.at[me],
            device_id=(group, target), device_id_type=MESH,
        )

    def y_arrived(source):
        pltpu.make_async_remote_copy(
            src_ref=y_all.at[source], dst_ref=y_all.at[source],
            send_sem=y_send.at[source], recv_sem=y_recv.at[source],
            device_id=(group, across), device_id_type=MESH,
        ).wait_recv()

    def small_copy(buf, send, recv, source, target):
        return pltpu.make_async_remote_copy(
            src_ref=buf.at[source], dst_ref=buf.at[source],
            send_sem=send.at[target], recv_sem=recv.at[source],
            device_id=(group, target), device_id_type=MESH,
        )

    def loop(low, high, body):
        def step(j, carry):
            body(j)
            return carry
        lax.fori_loop(low, high, step, 0)

    def others(body):
        loop(1, n, lambda j: body(lax.rem(me + j, n)))

    def y_send_row(p, r):
        loop(0, CORES, lambda j: y_copy(slot_of(p, r, lax.rem(core + j, CORES))).start())

    def y_send_planes(count, plane_at):
        def one(j):
            y_send_row(plane_at(j // ROWS), lax.rem(row + j, ROWS))
        loop(0, ROWS * count, one)

    def sides(k, body):
        def one(side):
            p = plane + k * (2 * side - 1)
            @pl.when((p >= 0) & (p < planes))
            def _():
                body(p)
        loop(0, 2, one)

    def from_across(p):
        slot = slot_of(p, 1 - row, core)
        for part in range(PARTS):
            x_arrived(slot, part)
            x_forward(slot, 3, partner, part)

    def from_line(p):
        slot = slot_of(p, row, core)
        for part in range(PARTS):
            x_arrived(slot, part)

            @pl.when((p < plane) & has_up)
            def _():
                x_forward(slot, 0, up, part)

            @pl.when((p > plane) & has_down)
            def _():
                x_forward(slot, 1, down, part)

            x_forward(slot, 2, across, part)
            x_forward(slot, 3, partner, part)

    def lines(k):
        sides(k, from_line)

        @pl.when((plane == k) & has_up)
        def _():
            y_send_planes(planes - 1 - plane, lambda j: plane + 1 + j)

        @pl.when((planes - 1 - plane == k) & has_down)
        def _():
            y_send_planes(plane, lambda j: plane - 1 - j)

    own_columns = pl.ds(pl.multiple_of(me * width_out, width_out), width_out)
    own_out = pl.ds(me * out_blocks, out_blocks)
    loads = [
        pltpu.make_async_copy(eigen_ref, eigen, local_sem.at[0]),
        pltpu.make_async_copy(query_ref, query, local_sem.at[1]),
        pltpu.make_async_copy(outb_ref.at[own_out], outb, local_sem.at[2]),
        pltpu.make_async_copy(inb_ref, inb, local_sem.at[3]),
        pltpu.make_async_copy(x_ref, x_all.at[me], local_sem.at[4]),
        pltpu.make_async_copy(y_ref.at[:, own_columns], y_all.at[me], local_sem.at[5]),
    ]

    barrier = pltpu.get_barrier_semaphore()

    def greet(semaphore, target):
        pl.semaphore_signal(semaphore, inc=1, device_id=(group, target), device_id_type=MESH)

    @pl.when(has_up)
    def _():
        greet(barrier, up)

    @pl.when(has_down)
    def _():
        greet(barrier, down)

    greet(barrier, across)
    greet(barrier, partner)
    for load in loads:
        load.start()
    pl.semaphore_wait(barrier, 2 + has_up.astype(jnp.int32) + has_down.astype(jnp.int32))

    for part in range(PARTS):
        @pl.when(has_up)
        def _():
            x_copy(x_ref, me, 0, up, part).start()

        @pl.when(has_down)
        def _():
            x_copy(x_ref, me, 1, down, part).start()

        x_copy(x_ref, me, 2, across, part).start()
        x_copy(x_ref, me, 3, partner, part).start()

    greet(plane_in, partner)
    y_copy(partner).start()
    pl.semaphore_wait(plane_in, 1)

    @pl.when(plane == 0)
    def _():
        greet(below_in, up)

    @pl.when(plane == planes - 1)
    def _():
        greet(above_in, down)

    loads[0].wait()

    def add_tile(b, carry):
        tile = eigen[b]
        folded = tile[:, :LANES]
        for lane in range(LANES, rows_in, LANES):
            folded = folded + tile[:, lane:lane + LANES]
        return carry + jnp.sum(folded.reshape(rows_out // 8, 8, LANES), axis=0)

    e_buf[me] = lax.fori_loop(0, tiles, add_tile, jnp.zeros((8, LANES), jnp.float32))

    @pl.when(has_down)
    def _():
        pl.semaphore_wait(below_in, 1)

        @pl.when(has_up)
        def _():
            greet(below_in, up)

    @pl.when(has_up)
    def _():
        pl.semaphore_wait(above_in, 1)

        @pl.when(has_down)
        def _():
            greet(above_in, down)

    others(lambda t: small_copy(e_buf, e_send, e_recv, me, t).start())

    @pl.when(at_end)
    def _():
        def outward(j):
            k = j + 1
            return jnp.where(plane == 0, k, planes - 1 - k)
        y_send_planes(planes - 1, outward)

    for load in loads[1:4]:
        load.wait()
    for j in range(out_blocks):
        outb_t[j] = outb[j].astype(jnp.float32).T.astype(jnp.bfloat16)

    def half_turn(b):
        for q in range(queries):
            for k in range(blocks_per_tile):
                lanes = slice(k * block, (k + 1) * block)
                query[b, q, :, lanes] = jnp.dot(
                    query[b, q, :, lanes], inb[b * blocks_per_tile + k],
                    preferred_element_type=jnp.float32,
                ).astype(jnp.bfloat16)

    loop(0, tiles, half_turn)
    lines(1)
    others(lambda t: small_copy(e_buf, e_send, e_recv, t, t).wait_recv())
    damping = 0.1 * (jnp.sum(e_buf[...]) / eigen_count)

    def finish(b):
        columns = pl.ds(pl.multiple_of(b * rows_in, rows_in), rows_in)
        for j in range(out_blocks):
            span = slice(j * block, (j + 1) * block)
            inverse = 1.0 / (eigen[b, span, :] + damping)
            for q in range(queries):
                turned = jnp.dot(outb_t[j], query[b, q, span, :], preferred_element_type=jnp.float32)
                pre[q * rows_out + j * block:q * rows_out + (j + 1) * block, columns] = (
                    turned * inverse
                ).astype(jnp.bfloat16)

    loop(0, tiles, finish)
    for load in loads[4:]:
        load.wait()
    acc[...] = jnp.zeros_like(acc)
    lanes_of_docs = acc.shape[1]
    rows = CORES * tokens
    docs = lengths_ref.shape[1]
    lengths[...] = jnp.zeros_like(lengths)
    lengths[0:1, 0:docs] = lengths_ref[...].astype(jnp.float32)
    lengths_row = lengths[0:1, :]
    lengths_down = jnp.broadcast_to(lengths_row, (lanes_of_docs, lanes_of_docs)).T
    earlier = lax.broadcasted_iota(jnp.int32, lengths_down.shape, 0)
    earlier = earlier <= lax.broadcasted_iota(jnp.int32, lengths_down.shape, 1)
    ends = jnp.sum(jnp.where(earlier, lengths_down, 0.0), axis=0, keepdims=True)
    lengths[1:2, :] = ends
    lengths[0:1, :] = ends - lengths_row

    def project_chip(p, r):
        base = slot_of(p, r, 0)
        for part in range(PARTS):
            x_arrived(base + 1 - core, part)
        for c in range(CORES):
            spot = slice(c * tokens, (c + 1) * tokens)
            for k in range(in_blocks):
                lanes = slice(k * block, (k + 1) * block)
                rotated[spot, lanes] = jnp.dot(
                    x_all[base + c, :, lanes], inb[k], preferred_element_type=jnp.float32
                ).astype(jnp.bfloat16)
        step = math.gcd(queries * rows_out, 256)
        for o in range(0, queries * rows_out, step):
            projected[p * ROWS + r, :, o:o + step] = lax.dot_general(
                rotated[...], pre[o:o + step, :], (((1,), (1,)), ((), ())),
                preferred_element_type=jnp.float32,
            )

    def tally_chip(p, r):
        base = slot_of(p, r, 0)
        for c in range(CORES):
            @pl.when(base + c != me)
            def _():
                y_arrived(base + c)
        for c in range(CORES):
            spot = slice(c * tokens, (c + 1) * tokens)
            for k in range(out_blocks):
                lanes = slice(k * block, (k + 1) * block)
                grads_rot[spot, lanes] = jnp.dot(
                    y_all[base + c, :, lanes], outb[k], preferred_element_type=jnp.float32
                ).astype(jnp.bfloat16).astype(jnp.float32)
        positions = base * tokens + lax.broadcasted_iota(jnp.int32, (rows, lanes_of_docs), 0)
        positions = positions.astype(jnp.float32)
        member = (positions >= lengths[0:1, :]) & (positions < lengths[1:2, :])
        for q in range(queries):
            total = jnp.zeros((rows, LANES), jnp.float32)
            for lane in range(0, rows_out, LANES):
                total = total + (
                    projected[p * ROWS + r, :, q * rows_out + lane:q * rows_out + lane + LANES]
                    * grads_rot[:, lane:lane + LANES]
                )
            score = jnp.sum(total, axis=1, keepdims=True)
            added = jnp.sum(jnp.where(member, score, 0.0), axis=0, keepdims=True)
            acc[q:q + 1, :] = acc[q:q + 1, :] + added

    def project_plane(p):
        from_across(p)
        loop(0, ROWS, lambda r: project_chip(p, lax.rem(row + r, ROWS)))

    project_plane(plane)
    loop(2, planes, lines)

    y_copy(across).start()
    y_copy(slot_of(plane, 1 - row, 1 - core)).start()
    loop(1, planes, lambda k: sides(k, project_plane))
    turn = jnp.where(2 * plane < planes, planes - 1, 1)

    def tally_plane(j):
        p = lax.rem(plane + turn * j, planes)
        loop(0, ROWS, lambda r: tally_chip(p, lax.rem(row + r, ROWS)))

    loop(0, planes, tally_plane)
    f_buf[me] = acc[...]
    others(lambda t: small_copy(f_buf, f_send, f_recv, me, t).start())

    def left(slot, channel):
        for part in range(PARTS):
            x_copy(x_all.at[slot], slot, channel, across, part).wait_send()

    def drain(p):
        slot = slot_of(p, row, core)

        @pl.when((p <= plane) & has_up)
        def _():
            left(slot, 0)

        @pl.when((p >= plane) & has_down)
        def _():
            left(slot, 1)

        left(slot, 2)
        left(slot, 3)
        left(slot_of(p, 1 - row, core), 3)

    loop(0, planes, drain)
    others(lambda t: y_copy(t).wait_send())
    others(lambda t: small_copy(e_buf, e_send, e_recv, me, t).wait_send())
    others(lambda t: small_copy(f_buf, f_send, f_recv, t, t).wait_recv())
    others(lambda t: small_copy(f_buf, f_send, f_recv, me, t).wait_send())
    summed = jnp.sum(f_buf[...], axis=0)
    lane = lax.broadcasted_iota(jnp.int32, summed.shape, 1)
    per_device = out_ref.shape[0]
    for j in range(per_device):
        picked = jnp.sum(jnp.where(lane == me * per_device + j, summed, 0.0), axis=1, keepdims=True)
        for q in range(queries):
            out_ref[j:j + 1, q:q + 1] = picked[q:q + 1, :]


def fused(n, layer_inputs, output_grads, query_grads, eigenvalues, out_basis, in_basis, doc_lengths):
    tokens, width_in = layer_inputs.shape
    tiles, queries, rows_out, rows_in = query_grads.shape
    docs = doc_lengths.shape[0]
    block = out_basis.shape[1]
    anyspace = pl.BlockSpec(memory_space=pl.ANY)
    vmem = pl.BlockSpec(memory_space=pltpu.VMEM)
    bf16, f32 = jnp.bfloat16, jnp.float32
    return pl.pallas_call(
        functools.partial(fused_kernel, n, output_grads.shape[1] * width_in),
        out_shape=jax.ShapeDtypeStruct((docs // n, queries), f32),
        in_specs=[anyspace] * 6 + [vmem],
        out_specs=vmem,
        scratch_shapes=[
            pltpu.VMEM((n, tokens, width_in), bf16),
            pltpu.VMEM((n, tokens, rows_out), bf16),
            pltpu.VMEM(query_grads.shape, bf16),
            pltpu.VMEM(eigenvalues.shape, f32),
            pltpu.VMEM((rows_out // block, block, block), bf16),
            pltpu.VMEM(in_basis.shape, bf16),
            pltpu.VMEM((rows_out // block, block, block), bf16),
            pltpu.VMEM((queries * rows_out, width_in), bf16),
            pltpu.VMEM((CORES * tokens, width_in), bf16),
            pltpu.VMEM((CORES * tokens, rows_out), f32),
            pltpu.VMEM((n // CORES, CORES * tokens, queries * rows_out), f32),
            pltpu.VMEM((8, LANES), f32),
            pltpu.VMEM((n, 8, LANES), f32),
            pltpu.VMEM((n, 8, LANES), f32),
            pltpu.VMEM((8, LANES), f32),
            pltpu.SemaphoreType.DMA((6,)),
            pltpu.SemaphoreType.DMA((n * PARTS, 4)),
            pltpu.SemaphoreType.DMA((n * PARTS,)),
        ] + [pltpu.SemaphoreType.DMA((n,))] * 6 + [pltpu.SemaphoreType.REGULAR] * 3,
        compiler_params=pltpu.CompilerParams(
            collective_id=0, has_side_effects=True, vmem_limit_bytes=60 * 1024 * 1024
        ),
    )(layer_inputs, output_grads, query_grads, eigenvalues, out_basis, in_basis, doc_lengths[None])


def local(n, *arrays):
    layer_inputs, output_grads, query_grads, _, _, _, doc_lengths = arrays
    tiles, queries, rows_out, rows_in = query_grads.shape
    whole_rows = tiles * rows_in == layer_inputs.shape[1] and n * rows_out == output_grads.shape[1]
    fits = n * layer_inputs.size <= 8 * query_grads.size and doc_lengths.shape[0] <= LANES
    shaped = n % (CORES * ROWS) == 0 and doc_lengths.shape[0] % n == 0 and queries <= 8
    shaped = shaped and layer_inputs.shape[0] % (16 * PARTS) == 0 and n > CORES * ROWS
    if whole_rows and fits and shaped:
        return fused(n, *arrays)
    return tiles_apart(*arrays)


def solution(mesh):
    in_specs = (
        P(("groups", "dp"), None),
        P(("groups", "dp"), None),
        P("dp", None, None, None),
        P("dp", None, None),
        P(),
        P(),
        P("groups"),
    )
    out_specs = P(("groups", "dp"), None)
    return jax.shard_map(functools.partial(local, mesh.shape["dp"]), mesh=mesh, in_specs=in_specs, out_specs=out_specs, check_vma=False)
```

```python
import functools
import math

import jax
import jax.numpy as jnp
from jax import lax
from jax.experimental import pallas as pl
from jax.experimental.pallas import tpu as pltpu
from jax.sharding import PartitionSpec as P


def turn_rows(columns, basis_blocks):
    group_count = basis_blocks.shape[0]
    block_width = basis_blocks.shape[1]
    grouped = columns.reshape(columns.shape[0], group_count, block_width)
    turned = jnp.einsum("tnk,nkj->tnj", grouped, basis_blocks, preferred_element_type=jnp.float32)
    return turned.reshape(columns.shape).astype(jnp.bfloat16)


def precondition(query_grads, eigenvalues, damping, tile_out, tile_in):
    blocks, queries, rows_out, rows_in = query_grads.shape
    block_width = tile_in.shape[-1]
    grouped = query_grads.reshape(blocks, queries, rows_out, rows_in // block_width, block_width)
    half_turned = jnp.einsum(
        "bqonk,bnkj->bqonj", grouped, tile_in, preferred_element_type=jnp.float32
    )
    half_turned = half_turned.reshape(blocks, queries, rows_out, rows_in).astype(jnp.bfloat16)
    grouped = half_turned.reshape(blocks, queries, rows_out // block_width, block_width, rows_in)
    turned = jnp.einsum("bqnki,bnkj->bqnji", grouped, tile_out, preferred_element_type=jnp.float32)
    turned = turned.reshape(blocks, queries, rows_out, rows_in)
    return (turned / (eigenvalues[:, None] + damping)).astype(jnp.bfloat16)


def tally_scores(grads_got, inputs_got, preconditioned, doc_starts, doc_ends):
    blocks, total_rows, rows_out = grads_got.shape
    queries = preconditioned.shape[1]
    row_step = math.gcd(1024, total_rows)
    flat_pre = preconditioned.reshape(blocks, queries * rows_out, preconditioned.shape[3])

    def one_piece(running, piece_index):
        start_row = piece_index * row_step
        grads_piece = lax.dynamic_slice_in_dim(grads_got, start_row, row_step, 1)
        inputs_piece = lax.dynamic_slice_in_dim(inputs_got, start_row, row_step, 1)
        projected = jnp.einsum(
            "bti,bpi->btp", inputs_piece, flat_pre, preferred_element_type=jnp.float32
        )
        projected = projected.reshape(blocks, row_step, queries, rows_out)
        scores = jnp.sum(projected * grads_piece[:, :, None, :].astype(jnp.float32), axis=(0, 3))
        positions = start_row + lax.iota(jnp.int32, row_step)
        member = (
            (positions[:, None] >= doc_starts[None, :]) & (positions[:, None] < doc_ends[None, :])
        ).astype(jnp.float32)
        added = jnp.einsum("td,tq->dq", member, scores, precision=lax.Precision.HIGHEST)
        return (running + added, None)

    initial = jnp.zeros((doc_starts.shape[0], queries), jnp.float32)
    summed, _ = lax.scan(one_piece, initial, jnp.arange(total_rows // row_step, dtype=jnp.int32))
    return summed


def tiles_apart(layer_inputs, output_grads, query_grads, eigenvalues, out_basis, in_basis, doc_lengths):
    block_width = out_basis.shape[1]
    tok_count = layer_inputs.shape[0]
    tile_count = query_grads.shape[0]
    rows_out = query_grads.shape[2]
    rows_in = query_grads.shape[3]
    in_tiles = layer_inputs.shape[1] // rows_in
    out_tiles = output_grads.shape[1] // rows_out
    tile_ids = lax.axis_index("dp") * tile_count + lax.iota(jnp.int32, tile_count)
    out_sets = out_basis.reshape(out_tiles, rows_out // block_width, block_width, block_width)
    in_sets = in_basis.reshape(in_tiles, rows_in // block_width, block_width, block_width)
    tile_out = jnp.take(out_sets, tile_ids // in_tiles, axis=0)
    tile_in = jnp.take(in_sets, tile_ids % in_tiles, axis=0)
    eigen_sum = lax.psum(jnp.sum(eigenvalues), "dp")
    entries = output_grads.shape[1] * layer_inputs.shape[1]
    damping = 0.1 * (eigen_sum / entries)
    preconditioned = precondition(query_grads, eigenvalues, damping, tile_out, tile_in)
    grads_local = turn_rows(output_grads, out_basis)
    inputs_local = turn_rows(layer_inputs, in_basis)
    grads_tiles = grads_local.reshape(tok_count, out_tiles, rows_out).transpose(1, 0, 2)[:, None]
    grads_tiles = jnp.broadcast_to(grads_tiles, (out_tiles, in_tiles, tok_count, rows_out))
    grads_tiles = grads_tiles.reshape(out_tiles * in_tiles, tok_count, rows_out)
    inputs_tiles = inputs_local.reshape(tok_count, in_tiles, rows_in).transpose(1, 0, 2)[None]
    inputs_tiles = jnp.broadcast_to(inputs_tiles, (out_tiles, in_tiles, tok_count, rows_in))
    inputs_tiles = inputs_tiles.reshape(out_tiles * in_tiles, tok_count, rows_in)
    grads_got, inputs_got = (
        lax.all_to_all(grads_tiles, "dp", split_axis=0, concat_axis=1, tiled=True),
        lax.all_to_all(inputs_tiles, "dp", split_axis=0, concat_axis=1, tiled=True),
    )
    doc_ends = jnp.cumsum(doc_lengths)
    doc_starts = doc_ends - doc_lengths
    partial_scores = tally_scores(grads_got, inputs_got, preconditioned, doc_starts, doc_ends)
    return lax.psum_scatter(partial_scores, "dp", scatter_dimension=0, tiled=True)


CORES = 2
ROWS = 2
PARTS = 2
LANES = 128
MESH = pl.DeviceIdType.MESH


def fused_kernel(
    n, eigen_count,
    x_ref, y_ref, query_ref, eigen_ref, outb_ref, inb_ref, lengths_ref,
    out_ref,
    x_all, y_all, query, eigen, outb, inb, outb_t, pre, rotated, grads_rot, projected, lengths, e_buf, f_buf, acc,
    local_sem, x_send, x_recv, y_send, y_recv, e_send, e_recv, f_send, f_recv, plane_in, below_in, above_in,
):
    planes = n // (CORES * ROWS)
    group, me = lax.axis_index("groups"), lax.axis_index("dp")
    core = lax.rem(me, CORES)
    row = lax.rem(me // CORES, ROWS)
    plane = me // (CORES * ROWS)
    tokens, width_in = x_ref.shape
    width_out = y_all.shape[2]
    tiles, queries, rows_out, rows_in = query_ref.shape
    block = outb_ref.shape[1]
    out_blocks = rows_out // block
    in_blocks = width_in // block
    blocks_per_tile = rows_in // block

    def slot_of(p, r, c):
        return (p * ROWS + r) * CORES + c

    up, down = me + CORES * ROWS, me - CORES * ROWS
    across = slot_of(plane, 1 - row, core)
    partner = slot_of(plane, row, 1 - core)
    has_up, has_down = plane < planes - 1, plane > 0
    at_end = (plane == 0) | (plane == planes - 1)

    def x_copy(src, slot, channel, target, part):
        span = pl.ds(part * (tokens // PARTS), tokens // PARTS)
        return pltpu.make_async_remote_copy(
            src_ref=src.at[span], dst_ref=x_all.at[slot, span],
            send_sem=x_send.at[slot * PARTS + part, channel],
            recv_sem=x_recv.at[slot * PARTS + part],
            device_id=(group, target), device_id_type=MESH,
        )

    def x_arrived(slot, part):
        x_copy(x_all.at[slot], slot, 0, across, part).wait_recv()

    def x_forward(slot, channel, target, part):
        x_copy(x_all.at[slot], slot, channel, target, part).start()

    def y_copy(target):
        columns = pl.ds(pl.multiple_of(target * width_out, width_out), width_out)
        return pltpu.make_async_remote_copy(
            src_ref=y_ref.at[:, columns], dst_ref=y_all.at[me],
            send_sem=y_send, recv_sem=y_recv.at[me],
            device_id=(group, target), device_id_type=MESH,
        )

    def y_arrived(source):
        pltpu.make_async_remote_copy(
            src_ref=y_all.at[source], dst_ref=y_all.at[source],
            send_sem=y_send, recv_sem=y_recv.at[source],
            device_id=(group, across), device_id_type=MESH,
        ).wait_recv()

    def small_copy(buf, send, recv, source, target):
        return pltpu.make_async_remote_copy(
            src_ref=buf.at[source], dst_ref=buf.at[source],
            send_sem=send, recv_sem=recv,
            device_id=(group, target), device_id_type=MESH,
        )

    def all_sent(buf, send):
        every = buf.at[pl.ds(0, n - 1)]
        pltpu.make_async_copy(every, every, send).wait()

    def loop(low, high, body):
        def step(j, carry):
            body(j)
            return carry
        lax.fori_loop(low, high, step, 0)

    def others(body):
        loop(1, n, lambda j: body(lax.rem(me + j, n)))

    def y_send_row(p, r):
        loop(0, CORES, lambda j: y_copy(slot_of(p, r, lax.rem(core + j, CORES))).start())

    def y_send_planes(count, plane_at):
        def one(j):
            y_send_row(plane_at(j // ROWS), lax.rem(row + j, ROWS))
        loop(0, ROWS * count, one)

    def sides(k, body):
        def one(side):
            p = plane + k * (2 * side - 1)
            @pl.when((p >= 0) & (p < planes))
            def _():
                body(p)
        loop(0, 2, one)

    def from_across(p):
        slot = slot_of(p, 1 - row, core)
        for part in range(PARTS):
            x_arrived(slot, part)
            x_forward(slot, 3, partner, part)

    def from_line(p):
        slot = slot_of(p, row, core)
        for part in range(PARTS):
            x_arrived(slot, part)

            @pl.when((p < plane) & has_up)
            def _():
                x_forward(slot, 0, up, part)

            @pl.when((p > plane) & has_down)
            def _():
                x_forward(slot, 1, down, part)

            x_forward(slot, 2, across, part)
            x_forward(slot, 3, partner, part)

    def lines(k):
        sides(k, from_line)

        @pl.when((plane == k) & has_up)
        def _():
            y_send_planes(planes - 1 - plane, lambda j: plane + 1 + j)

        @pl.when((planes - 1 - plane == k) & has_down)
        def _():
            y_send_planes(plane, lambda j: plane - 1 - j)

    own_columns = pl.ds(pl.multiple_of(me * width_out, width_out), width_out)
    own_out = pl.ds(me * out_blocks, out_blocks)
    loads = [
        pltpu.make_async_copy(eigen_ref, eigen, local_sem.at[0]),
        pltpu.make_async_copy(query_ref, query, local_sem.at[1]),
        pltpu.make_async_copy(outb_ref.at[own_out], outb, local_sem.at[2]),
        pltpu.make_async_copy(inb_ref, inb, local_sem.at[3]),
        pltpu.make_async_copy(x_ref, x_all.at[me], local_sem.at[4]),
        pltpu.make_async_copy(y_ref.at[:, own_columns], y_all.at[me], local_sem.at[5]),
    ]

    barrier = pltpu.get_barrier_semaphore()

    def greet(semaphore, target):
        pl.semaphore_signal(semaphore, inc=1, device_id=(group, target), device_id_type=MESH)

    @pl.when(has_up)
    def _():
        greet(barrier, up)

    @pl.when(has_down)
    def _():
        greet(barrier, down)

    greet(barrier, across)
    greet(barrier, partner)
    for load in loads:
        load.start()
    pl.semaphore_wait(barrier, 2 + has_up.astype(jnp.int32) + has_down.astype(jnp.int32))

    for part in range(PARTS):
        @pl.when(has_up)
        def _():
            x_copy(x_ref, me, 0, up, part).start()

        @pl.when(has_down)
        def _():
            x_copy(x_ref, me, 1, down, part).start()

        x_copy(x_ref, me, 2, across, part).start()
        x_copy(x_ref, me, 3, partner, part).start()

    greet(plane_in, partner)
    y_copy(partner).start()
    pl.semaphore_wait(plane_in, 1)

    @pl.when(plane == 0)
    def _():
        greet(below_in, up)

    @pl.when(plane == planes - 1)
    def _():
        greet(above_in, down)

    loads[0].wait()

    def add_tile(b, carry):
        tile = eigen[b]
        folded = tile[:, :LANES]
        for lane in range(LANES, rows_in, LANES):
            folded = folded + tile[:, lane:lane + LANES]
        return carry + jnp.sum(folded.reshape(rows_out // 8, 8, LANES), axis=0)

    eigen_total = lax.fori_loop(0, tiles, add_tile, jnp.zeros((8, LANES), jnp.float32))
    e_buf[me] = jnp.sum(eigen_total, axis=0, keepdims=True)

    @pl.when(has_down)
    def _():
        pl.semaphore_wait(below_in, 1)

        @pl.when(has_up)
        def _():
            greet(below_in, up)

    @pl.when(has_up)
    def _():
        pl.semaphore_wait(above_in, 1)

        @pl.when(has_down)
        def _():
            greet(above_in, down)

    others(lambda t: small_copy(e_buf, e_send, e_recv, me, t).start())

    @pl.when(at_end)
    def _():
        def outward(j):
            k = j + 1
            return jnp.where(plane == 0, k, planes - 1 - k)
        y_send_planes(planes - 1, outward)

    for load in loads[1:4]:
        load.wait()
    for j in range(out_blocks):
        outb_t[j] = outb[j].astype(jnp.float32).T.astype(jnp.bfloat16)

    def half_turn(b):
        for q in range(queries):
            for k in range(blocks_per_tile):
                lanes = slice(k * block, (k + 1) * block)
                query[b, q, :, lanes] = jnp.dot(
                    query[b, q, :, lanes], inb[b * blocks_per_tile + k],
                    preferred_element_type=jnp.float32,
                ).astype(jnp.bfloat16)

    loop(0, tiles, half_turn)
    lines(1)
    all_sent(e_buf, e_recv)
    damping = 0.1 * (jnp.sum(e_buf[...]) / eigen_count)

    def finish(b):
        columns = pl.ds(pl.multiple_of(b * rows_in, rows_in), rows_in)
        for j in range(out_blocks):
            span = slice(j * block, (j + 1) * block)
            inverse = 1.0 / (eigen[b, span, :] + damping)
            for q in range(queries):
                turned = jnp.dot(outb_t[j], query[b, q, span, :], preferred_element_type=jnp.float32)
                pre[q * rows_out + j * block:q * rows_out + (j + 1) * block, columns] = (
                    turned * inverse
                ).astype(jnp.bfloat16)

    loop(0, tiles, finish)
    for load in loads[4:]:
        load.wait()
    acc[...] = jnp.zeros_like(acc)
    lanes_of_docs = acc.shape[1]
    rows = CORES * tokens
    docs = lengths_ref.shape[1]
    lengths[...] = jnp.zeros_like(lengths)
    lengths[0:1, 0:docs] = lengths_ref[...].astype(jnp.float32)
    lengths_row = lengths[0:1, :]
    lengths_down = jnp.broadcast_to(lengths_row, (lanes_of_docs, lanes_of_docs)).T
    earlier = lax.broadcasted_iota(jnp.int32, lengths_down.shape, 0)
    earlier = earlier <= lax.broadcasted_iota(jnp.int32, lengths_down.shape, 1)
    ends = jnp.sum(jnp.where(earlier, lengths_down, 0.0), axis=0, keepdims=True)
    lengths[1:2, :] = ends
    lengths[0:1, :] = ends - lengths_row

    def project_chip(p, r):
        base = slot_of(p, r, 0)
        for part in range(PARTS):
            x_arrived(base + 1 - core, part)
        for c in range(CORES):
            spot = slice(c * tokens, (c + 1) * tokens)
            for k in range(in_blocks):
                lanes = slice(k * block, (k + 1) * block)
                rotated[spot, lanes] = jnp.dot(
                    x_all[base + c, :, lanes], inb[k], preferred_element_type=jnp.float32
                ).astype(jnp.bfloat16)
        step = math.gcd(queries * rows_out, 256)
        for o in range(0, queries * rows_out, step):
            projected[p * ROWS + r, :, o:o + step] = lax.dot_general(
                rotated[...], pre[o:o + step, :], (((1,), (1,)), ((), ())),
                preferred_element_type=jnp.float32,
            )

    def tally_chip(p, r):
        base = slot_of(p, r, 0)
        for c in range(CORES):
            @pl.when(base + c != me)
            def _():
                y_arrived(base + c)
        for c in range(CORES):
            spot = slice(c * tokens, (c + 1) * tokens)
            for k in range(out_blocks):
                lanes = slice(k * block, (k + 1) * block)
                grads_rot[spot, lanes] = jnp.dot(
                    y_all[base + c, :, lanes], outb[k], preferred_element_type=jnp.float32
                ).astype(jnp.bfloat16).astype(jnp.float32)
        positions = base * tokens + lax.broadcasted_iota(jnp.int32, (rows, lanes_of_docs), 0)
        positions = positions.astype(jnp.float32)
        member = (positions >= lengths[0:1, :]) & (positions < lengths[1:2, :])
        for q in range(queries):
            total = jnp.zeros((rows, LANES), jnp.float32)
            for lane in range(0, rows_out, LANES):
                total = total + (
                    projected[p * ROWS + r, :, q * rows_out + lane:q * rows_out + lane + LANES]
                    * grads_rot[:, lane:lane + LANES]
                )
            score = jnp.sum(total, axis=1, keepdims=True)
            added = jnp.sum(jnp.where(member, score, 0.0), axis=0, keepdims=True)
            acc[q:q + 1, :] = acc[q:q + 1, :] + added

    def project_plane(p):
        from_across(p)
        loop(0, ROWS, lambda r: project_chip(p, lax.rem(row + r, ROWS)))

    project_plane(plane)
    loop(2, planes, lines)

    y_copy(across).start()
    y_copy(slot_of(plane, 1 - row, 1 - core)).start()
    loop(1, planes, lambda k: sides(k, project_plane))
    turn = jnp.where(2 * plane < planes, planes - 1, 1)

    def tally_plane(j):
        p = lax.rem(plane + turn * j, planes)
        loop(0, ROWS, lambda r: tally_chip(p, lax.rem(row + r, ROWS)))

    loop(0, planes, tally_plane)
    f_buf[me] = acc[0:queries, :]
    others(lambda t: small_copy(f_buf, f_send, f_recv, me, t).start())

    def left(slot, channel):
        for part in range(PARTS):
            x_copy(x_all.at[slot], slot, channel, across, part).wait_send()

    def drain(p):
        slot = slot_of(p, row, core)

        @pl.when((p <= plane) & has_up)
        def _():
            left(slot, 0)

        @pl.when((p >= plane) & has_down)
        def _():
            left(slot, 1)

        left(slot, 2)
        left(slot, 3)
        left(slot_of(p, 1 - row, core), 3)

    loop(0, planes, drain)
    all_sent(y_all, y_send)
    all_sent(e_buf, e_send)
    all_sent(f_buf, f_recv)
    all_sent(f_buf, f_send)
    summed = jnp.sum(f_buf[...], axis=0)
    lane = lax.broadcasted_iota(jnp.int32, summed.shape, 1)
    per_device = out_ref.shape[0]
    for j in range(per_device):
        picked = jnp.sum(jnp.where(lane == me * per_device + j, summed, 0.0), axis=1, keepdims=True)
        for q in range(queries):
            out_ref[j:j + 1, q:q + 1] = picked[q:q + 1, :]


def fused(n, layer_inputs, output_grads, query_grads, eigenvalues, out_basis, in_basis, doc_lengths):
    tokens, width_in = layer_inputs.shape
    tiles, queries, rows_out, rows_in = query_grads.shape
    docs = doc_lengths.shape[0]
    block = out_basis.shape[1]
    anyspace = pl.BlockSpec(memory_space=pl.ANY)
    vmem = pl.BlockSpec(memory_space=pltpu.VMEM)
    bf16, f32 = jnp.bfloat16, jnp.float32
    return pl.pallas_call(
        functools.partial(fused_kernel, n, output_grads.shape[1] * width_in),
        out_shape=jax.ShapeDtypeStruct((docs // n, queries), f32),
        in_specs=[anyspace] * 6 + [vmem],
        out_specs=vmem,
        scratch_shapes=[
            pltpu.VMEM((n, tokens, width_in), bf16),
            pltpu.VMEM((n, tokens, rows_out), bf16),
            pltpu.VMEM(query_grads.shape, bf16),
            pltpu.VMEM(eigenvalues.shape, f32),
            pltpu.VMEM((rows_out // block, block, block), bf16),
            pltpu.VMEM(in_basis.shape, bf16),
            pltpu.VMEM((rows_out // block, block, block), bf16),
            pltpu.VMEM((queries * rows_out, width_in), bf16),
            pltpu.VMEM((CORES * tokens, width_in), bf16),
            pltpu.VMEM((CORES * tokens, rows_out), f32),
            pltpu.VMEM((n // CORES, CORES * tokens, queries * rows_out), f32),
            pltpu.VMEM((8, LANES), f32),
            pltpu.VMEM((n, 1, LANES), f32),
            pltpu.VMEM((n, queries, LANES), f32),
            pltpu.VMEM((8, LANES), f32),
            pltpu.SemaphoreType.DMA((6,)),
            pltpu.SemaphoreType.DMA((n * PARTS, 4)),
            pltpu.SemaphoreType.DMA((n * PARTS,)),
            pltpu.SemaphoreType.DMA,
            pltpu.SemaphoreType.DMA((n,)),
        ] + [pltpu.SemaphoreType.DMA] * 4 + [pltpu.SemaphoreType.REGULAR] * 3,
        compiler_params=pltpu.CompilerParams(
            collective_id=0, has_side_effects=True, vmem_limit_bytes=60 * 1024 * 1024
        ),
    )(layer_inputs, output_grads, query_grads, eigenvalues, out_basis, in_basis, doc_lengths[None])


def local(n, *arrays):
    layer_inputs, output_grads, query_grads, _, _, _, doc_lengths = arrays
    tiles, queries, rows_out, rows_in = query_grads.shape
    whole_rows = tiles * rows_in == layer_inputs.shape[1] and n * rows_out == output_grads.shape[1]
    fits = n * layer_inputs.size <= 8 * query_grads.size and doc_lengths.shape[0] <= LANES
    shaped = n % (CORES * ROWS) == 0 and doc_lengths.shape[0] % n == 0 and queries <= 8
    shaped = shaped and layer_inputs.shape[0] % (16 * PARTS) == 0 and n > CORES * ROWS
    if whole_rows and fits and shaped:
        return fused(n, *arrays)
    return tiles_apart(*arrays)


def solution(mesh):
    in_specs = (
        P(("groups", "dp"), None),
        P(("groups", "dp"), None),
        P("dp", None, None, None),
        P("dp", None, None),
        P(),
        P(),
        P("groups"),
    )
    out_specs = P(("groups", "dp"), None)
    return jax.shard_map(functools.partial(local, mesh.shape["dp"]), mesh=mesh, in_specs=in_specs, out_specs=out_specs, check_vma=False)
```

```python
import functools
import math

import jax
import jax.numpy as jnp
from jax import lax
from jax.experimental import pallas as pl
from jax.experimental.pallas import tpu as pltpu
from jax.sharding import PartitionSpec as P


def turn_rows(columns, basis_blocks):
    group_count = basis_blocks.shape[0]
    block_width = basis_blocks.shape[1]
    grouped = columns.reshape(columns.shape[0], group_count, block_width)
    turned = jnp.einsum("tnk,nkj->tnj", grouped, basis_blocks, preferred_element_type=jnp.float32)
    return turned.reshape(columns.shape).astype(jnp.bfloat16)


def precondition(query_grads, eigenvalues, damping, tile_out, tile_in):
    blocks, queries, rows_out, rows_in = query_grads.shape
    block_width = tile_in.shape[-1]
    grouped = query_grads.reshape(blocks, queries, rows_out, rows_in // block_width, block_width)
    half_turned = jnp.einsum(
        "bqonk,bnkj->bqonj", grouped, tile_in, preferred_element_type=jnp.float32
    )
    half_turned = half_turned.reshape(blocks, queries, rows_out, rows_in).astype(jnp.bfloat16)
    grouped = half_turned.reshape(blocks, queries, rows_out // block_width, block_width, rows_in)
    turned = jnp.einsum("bqnki,bnkj->bqnji", grouped, tile_out, preferred_element_type=jnp.float32)
    turned = turned.reshape(blocks, queries, rows_out, rows_in)
    return (turned / (eigenvalues[:, None] + damping)).astype(jnp.bfloat16)


def tally_scores(grads_got, inputs_got, preconditioned, doc_starts, doc_ends):
    blocks, total_rows, rows_out = grads_got.shape
    queries = preconditioned.shape[1]
    row_step = math.gcd(1024, total_rows)
    flat_pre = preconditioned.reshape(blocks, queries * rows_out, preconditioned.shape[3])

    def one_piece(running, piece_index):
        start_row = piece_index * row_step
        grads_piece = lax.dynamic_slice_in_dim(grads_got, start_row, row_step, 1)
        inputs_piece = lax.dynamic_slice_in_dim(inputs_got, start_row, row_step, 1)
        projected = jnp.einsum(
            "bti,bpi->btp", inputs_piece, flat_pre, preferred_element_type=jnp.float32
        )
        projected = projected.reshape(blocks, row_step, queries, rows_out)
        scores = jnp.sum(projected * grads_piece[:, :, None, :].astype(jnp.float32), axis=(0, 3))
        positions = start_row + lax.iota(jnp.int32, row_step)
        member = (
            (positions[:, None] >= doc_starts[None, :]) & (positions[:, None] < doc_ends[None, :])
        ).astype(jnp.float32)
        added = jnp.einsum("td,tq->dq", member, scores, precision=lax.Precision.HIGHEST)
        return (running + added, None)

    initial = jnp.zeros((doc_starts.shape[0], queries), jnp.float32)
    summed, _ = lax.scan(one_piece, initial, jnp.arange(total_rows // row_step, dtype=jnp.int32))
    return summed


def tiles_apart(layer_inputs, output_grads, query_grads, eigenvalues, out_basis, in_basis, doc_lengths):
    block_width = out_basis.shape[1]
    tok_count = layer_inputs.shape[0]
    tile_count = query_grads.shape[0]
    rows_out = query_grads.shape[2]
    rows_in = query_grads.shape[3]
    in_tiles = layer_inputs.shape[1] // rows_in
    out_tiles = output_grads.shape[1] // rows_out
    tile_ids = lax.axis_index("dp") * tile_count + lax.iota(jnp.int32, tile_count)
    out_sets = out_basis.reshape(out_tiles, rows_out // block_width, block_width, block_width)
    in_sets = in_basis.reshape(in_tiles, rows_in // block_width, block_width, block_width)
    tile_out = jnp.take(out_sets, tile_ids // in_tiles, axis=0)
    tile_in = jnp.take(in_sets, tile_ids % in_tiles, axis=0)
    eigen_sum = lax.psum(jnp.sum(eigenvalues), "dp")
    entries = output_grads.shape[1] * layer_inputs.shape[1]
    damping = 0.1 * (eigen_sum / entries)
    preconditioned = precondition(query_grads, eigenvalues, damping, tile_out, tile_in)
    grads_local = turn_rows(output_grads, out_basis)
    inputs_local = turn_rows(layer_inputs, in_basis)
    grads_tiles = grads_local.reshape(tok_count, out_tiles, rows_out).transpose(1, 0, 2)[:, None]
    grads_tiles = jnp.broadcast_to(grads_tiles, (out_tiles, in_tiles, tok_count, rows_out))
    grads_tiles = grads_tiles.reshape(out_tiles * in_tiles, tok_count, rows_out)
    inputs_tiles = inputs_local.reshape(tok_count, in_tiles, rows_in).transpose(1, 0, 2)[None]
    inputs_tiles = jnp.broadcast_to(inputs_tiles, (out_tiles, in_tiles, tok_count, rows_in))
    inputs_tiles = inputs_tiles.reshape(out_tiles * in_tiles, tok_count, rows_in)
    grads_got, inputs_got = (
        lax.all_to_all(grads_tiles, "dp", split_axis=0, concat_axis=1, tiled=True),
        lax.all_to_all(inputs_tiles, "dp", split_axis=0, concat_axis=1, tiled=True),
    )
    doc_ends = jnp.cumsum(doc_lengths)
    doc_starts = doc_ends - doc_lengths
    partial_scores = tally_scores(grads_got, inputs_got, preconditioned, doc_starts, doc_ends)
    return lax.psum_scatter(partial_scores, "dp", scatter_dimension=0, tiled=True)


CORES = 2
ROWS = 2
PARTS = 2
LANES = 128
MESH = pl.DeviceIdType.MESH


def fused_kernel(
    n, eigen_count,
    x_ref, y_ref, query_ref, eigen_ref, outb_ref, inb_ref, lengths_ref,
    out_ref,
    x_all, y_all, query, eigen, outb, inb, outb_t, pre, rotated, grads_rot, projected, lengths, e_buf, f_buf, acc,
    local_sem, x_send, x_recv, y_send, y_recv, e_send, e_recv, f_send, f_recv, plane_in, below_in, above_in,
):
    planes = n // (CORES * ROWS)
    group, me = lax.axis_index("groups"), lax.axis_index("dp")
    core = lax.rem(me, CORES)
    row = lax.rem(me // CORES, ROWS)
    plane = me // (CORES * ROWS)
    tokens, width_in = x_ref.shape
    width_out = y_all.shape[2]
    tiles, queries, rows_out, rows_in = query_ref.shape
    block = outb_ref.shape[1]
    out_blocks = rows_out // block
    in_blocks = width_in // block
    blocks_per_tile = rows_in // block

    def slot_of(p, r, c):
        return (p * ROWS + r) * CORES + c

    up, down = me + CORES * ROWS, me - CORES * ROWS
    across = slot_of(plane, 1 - row, core)
    partner = slot_of(plane, row, 1 - core)
    has_up, has_down = plane < planes - 1, plane > 0
    at_end = (plane == 0) | (plane == planes - 1)

    def x_copy(src, slot, channel, target, part):
        span = pl.ds(part * (tokens // PARTS), tokens // PARTS)
        return pltpu.make_async_remote_copy(
            src_ref=src.at[span], dst_ref=x_all.at[slot, span],
            send_sem=x_send.at[slot * PARTS + part, channel],
            recv_sem=x_recv.at[slot * PARTS + part],
            device_id=(group, target), device_id_type=MESH,
        )

    def x_arrived(slot, part):
        x_copy(x_all.at[slot], slot, 0, across, part).wait_recv()

    def x_forward(slot, channel, target, part):
        x_copy(x_all.at[slot], slot, channel, target, part).start()

    def y_copy(target):
        columns = pl.ds(pl.multiple_of(target * width_out, width_out), width_out)
        return pltpu.make_async_remote_copy(
            src_ref=y_ref.at[:, columns], dst_ref=y_all.at[me],
            send_sem=y_send, recv_sem=y_recv.at[me],
            device_id=(group, target), device_id_type=MESH,
        )

    def y_arrived(source):
        pltpu.make_async_remote_copy(
            src_ref=y_all.at[source], dst_ref=y_all.at[source],
            send_sem=y_send, recv_sem=y_recv.at[source],
            device_id=(group, across), device_id_type=MESH,
        ).wait_recv()

    def small_copy(buf, send, recv, source, target):
        return pltpu.make_async_remote_copy(
            src_ref=buf.at[source], dst_ref=buf.at[source],
            send_sem=send, recv_sem=recv,
            device_id=(group, target), device_id_type=MESH,
        )

    def all_sent(buf, send):
        every = buf.at[pl.ds(0, n - 1)]
        pltpu.make_async_copy(every, every, send).wait()

    def loop(low, high, body):
        def step(j, carry):
            body(j)
            return carry
        lax.fori_loop(low, high, step, 0)

    def others(body):
        loop(1, n, lambda j: body(lax.rem(me + j, n)))

    def y_send_row(p, r):
        loop(0, CORES, lambda j: y_copy(slot_of(p, r, lax.rem(core + j, CORES))).start())

    def y_send_planes(count, plane_at):
        def one(j):
            y_send_row(plane_at(j // ROWS), lax.rem(row + j, ROWS))
        loop(0, ROWS * count, one)

    def sides(k, body):
        def one(side):
            p = plane + k * (2 * side - 1)
            @pl.when((p >= 0) & (p < planes))
            def _():
                body(p)
        loop(0, 2, one)

    def from_across(p):
        slot = slot_of(p, 1 - row, core)
        for part in range(PARTS):
            x_arrived(slot, part)
            x_forward(slot, 3, partner, part)

    def from_line(p):
        slot = slot_of(p, row, core)
        for part in range(PARTS):
            x_arrived(slot, part)

            @pl.when((p < plane) & has_up)
            def _():
                x_forward(slot, 0, up, part)

            @pl.when((p > plane) & has_down)
            def _():
                x_forward(slot, 1, down, part)

            x_forward(slot, 2, across, part)
            x_forward(slot, 3, partner, part)

    def lines(k):
        sides(k, from_line)

        @pl.when((plane == k) & has_up)
        def _():
            y_send_planes(planes - 1 - plane, lambda j: plane + 1 + j)

        @pl.when((planes - 1 - plane == k) & has_down)
        def _():
            y_send_planes(plane, lambda j: plane - 1 - j)

    own_columns = pl.ds(pl.multiple_of(me * width_out, width_out), width_out)
    own_out = pl.ds(me * out_blocks, out_blocks)
    loads = [
        pltpu.make_async_copy(eigen_ref, eigen, local_sem.at[0]),
        pltpu.make_async_copy(query_ref, query, local_sem.at[1]),
        pltpu.make_async_copy(outb_ref.at[own_out], outb, local_sem.at[2]),
        pltpu.make_async_copy(inb_ref, inb, local_sem.at[3]),
        pltpu.make_async_copy(x_ref, x_all.at[me], local_sem.at[4]),
        pltpu.make_async_copy(y_ref.at[:, own_columns], y_all.at[me], local_sem.at[5]),
    ]

    barrier = pltpu.get_barrier_semaphore()

    def greet(semaphore, target):
        pl.semaphore_signal(semaphore, inc=1, device_id=(group, target), device_id_type=MESH)

    @pl.when(has_up)
    def _():
        greet(barrier, up)

    @pl.when(has_down)
    def _():
        greet(barrier, down)

    greet(barrier, across)
    greet(barrier, partner)
    for load in loads:
        load.start()
    pl.semaphore_wait(barrier, 2 + has_up.astype(jnp.int32) + has_down.astype(jnp.int32))

    for part in range(PARTS):
        @pl.when(has_up)
        def _():
            x_copy(x_ref, me, 0, up, part).start()

        @pl.when(has_down)
        def _():
            x_copy(x_ref, me, 1, down, part).start()

        x_copy(x_ref, me, 2, across, part).start()
        x_copy(x_ref, me, 3, partner, part).start()

    greet(plane_in, partner)
    pl.semaphore_wait(plane_in, 1)

    @pl.when(plane == 0)
    def _():
        greet(below_in, up)

    @pl.when(plane == planes - 1)
    def _():
        greet(above_in, down)

    loads[0].wait()

    def add_tile(b, carry):
        tile = eigen[b]
        folded = tile[:, :LANES]
        for lane in range(LANES, rows_in, LANES):
            folded = folded + tile[:, lane:lane + LANES]
        return carry + jnp.sum(folded.reshape(rows_out // 8, 8, LANES), axis=0)

    eigen_total = lax.fori_loop(0, tiles, add_tile, jnp.zeros((8, LANES), jnp.float32))
    e_buf[me] = jnp.sum(eigen_total, axis=0, keepdims=True)

    @pl.when(has_down)
    def _():
        pl.semaphore_wait(below_in, 1)

        @pl.when(has_up)
        def _():
            greet(below_in, up)

    @pl.when(has_up)
    def _():
        pl.semaphore_wait(above_in, 1)

        @pl.when(has_down)
        def _():
            greet(above_in, down)

    others(lambda t: small_copy(e_buf, e_send, e_recv, me, t).start())

    @pl.when(at_end)
    def _():
        def outward(j):
            k = j + 1
            return jnp.where(plane == 0, k, planes - 1 - k)
        y_send_planes(planes - 1, outward)

    for load in loads[1:4]:
        load.wait()
    for j in range(out_blocks):
        outb_t[j] = outb[j].astype(jnp.float32).T.astype(jnp.bfloat16)

    def half_turn(b):
        for q in range(queries):
            for k in range(blocks_per_tile):
                lanes = slice(k * block, (k + 1) * block)
                query[b, q, :, lanes] = jnp.dot(
                    query[b, q, :, lanes], inb[b * blocks_per_tile + k],
                    preferred_element_type=jnp.float32,
                ).astype(jnp.bfloat16)

    loop(0, tiles, half_turn)
    lines(1)
    all_sent(e_buf, e_recv)
    damping = 0.1 * (jnp.sum(e_buf[...]) / eigen_count)

    def finish(b):
        columns = pl.ds(pl.multiple_of(b * rows_in, rows_in), rows_in)
        for j in range(out_blocks):
            span = slice(j * block, (j + 1) * block)
            inverse = 1.0 / (eigen[b, span, :] + damping)
            for q in range(queries):
                turned = jnp.dot(outb_t[j], query[b, q, span, :], preferred_element_type=jnp.float32)
                pre[q * rows_out + j * block:q * rows_out + (j + 1) * block, columns] = (
                    turned * inverse
                ).astype(jnp.bfloat16)

    loop(0, tiles, finish)
    for load in loads[4:]:
        load.wait()
    acc[...] = jnp.zeros_like(acc)
    lanes_of_docs = acc.shape[1]
    rows = CORES * tokens
    docs = lengths_ref.shape[1]
    lengths[...] = jnp.zeros_like(lengths)
    lengths[0:1, 0:docs] = lengths_ref[...].astype(jnp.float32)
    lengths_row = lengths[0:1, :]
    lengths_down = jnp.broadcast_to(lengths_row, (lanes_of_docs, lanes_of_docs)).T
    earlier = lax.broadcasted_iota(jnp.int32, lengths_down.shape, 0)
    earlier = earlier <= lax.broadcasted_iota(jnp.int32, lengths_down.shape, 1)
    ends = jnp.sum(jnp.where(earlier, lengths_down, 0.0), axis=0, keepdims=True)
    lengths[1:2, :] = ends
    lengths[0:1, :] = ends - lengths_row

    def project_chip(p, r):
        base = slot_of(p, r, 0)
        for part in range(PARTS):
            x_arrived(base + 1 - core, part)
        for c in range(CORES):
            spot = slice(c * tokens, (c + 1) * tokens)
            for k in range(in_blocks):
                lanes = slice(k * block, (k + 1) * block)
                rotated[spot, lanes] = jnp.dot(
                    x_all[base + c, :, lanes], inb[k], preferred_element_type=jnp.float32
                ).astype(jnp.bfloat16)
        step = math.gcd(queries * rows_out, 256)
        for o in range(0, queries * rows_out, step):
            projected[p * ROWS + r, :, o:o + step] = lax.dot_general(
                rotated[...], pre[o:o + step, :], (((1,), (1,)), ((), ())),
                preferred_element_type=jnp.float32,
            )

    def tally_chip(p, r):
        base = slot_of(p, r, 0)
        for c in range(CORES):
            @pl.when(base + c != me)
            def _():
                y_arrived(base + c)
        for c in range(CORES):
            spot = slice(c * tokens, (c + 1) * tokens)
            for k in range(out_blocks):
                lanes = slice(k * block, (k + 1) * block)
                grads_rot[spot, lanes] = jnp.dot(
                    y_all[base + c, :, lanes], outb[k], preferred_element_type=jnp.float32
                ).astype(jnp.bfloat16).astype(jnp.float32)
        positions = base * tokens + lax.broadcasted_iota(jnp.int32, (rows, lanes_of_docs), 0)
        positions = positions.astype(jnp.float32)
        member = (positions >= lengths[0:1, :]) & (positions < lengths[1:2, :])
        for q in range(queries):
            total = jnp.zeros((rows, LANES), jnp.float32)
            for lane in range(0, rows_out, LANES):
                total = total + (
                    projected[p * ROWS + r, :, q * rows_out + lane:q * rows_out + lane + LANES]
                    * grads_rot[:, lane:lane + LANES]
                )
            score = jnp.sum(total, axis=1, keepdims=True)
            added = jnp.sum(jnp.where(member, score, 0.0), axis=0, keepdims=True)
            acc[q:q + 1, :] = acc[q:q + 1, :] + added

    def project_plane(p):
        from_across(p)
        loop(0, ROWS, lambda r: project_chip(p, lax.rem(row + r, ROWS)))

    project_plane(plane)
    loop(2, planes, lines)

    y_copy(partner).start()
    y_copy(across).start()
    y_copy(slot_of(plane, 1 - row, 1 - core)).start()
    loop(1, planes, lambda k: sides(k, project_plane))
    turn = jnp.where(2 * plane < planes, planes - 1, 1)

    def tally_plane(j):
        p = lax.rem(plane + turn * j, planes)
        loop(0, ROWS, lambda r: tally_chip(p, lax.rem(row + r, ROWS)))

    loop(0, planes, tally_plane)
    f_buf[me] = acc[0:queries, :]
    others(lambda t: small_copy(f_buf, f_send, f_recv, me, t).start())

    def left(slot, channel):
        for part in range(PARTS):
            x_copy(x_all.at[slot], slot, channel, across, part).wait_send()

    def drain(p):
        slot = slot_of(p, row, core)

        @pl.when((p <= plane) & has_up)
        def _():
            left(slot, 0)

        @pl.when((p >= plane) & has_down)
        def _():
            left(slot, 1)

        left(slot, 2)
        left(slot, 3)
        left(slot_of(p, 1 - row, core), 3)

    loop(0, planes, drain)
    all_sent(y_all, y_send)
    all_sent(e_buf, e_send)
    all_sent(f_buf, f_recv)
    all_sent(f_buf, f_send)
    summed = jnp.sum(f_buf[...], axis=0)
    lane = lax.broadcasted_iota(jnp.int32, summed.shape, 1)
    per_device = out_ref.shape[0]
    for j in range(per_device):
        picked = jnp.sum(jnp.where(lane == me * per_device + j, summed, 0.0), axis=1, keepdims=True)
        for q in range(queries):
            out_ref[j:j + 1, q:q + 1] = picked[q:q + 1, :]


def fused(n, layer_inputs, output_grads, query_grads, eigenvalues, out_basis, in_basis, doc_lengths):
    tokens, width_in = layer_inputs.shape
    tiles, queries, rows_out, rows_in = query_grads.shape
    docs = doc_lengths.shape[0]
    block = out_basis.shape[1]
    anyspace = pl.BlockSpec(memory_space=pl.ANY)
    vmem = pl.BlockSpec(memory_space=pltpu.VMEM)
    bf16, f32 = jnp.bfloat16, jnp.float32
    return pl.pallas_call(
        functools.partial(fused_kernel, n, output_grads.shape[1] * width_in),
        out_shape=jax.ShapeDtypeStruct((docs // n, queries), f32),
        in_specs=[anyspace] * 6 + [vmem],
        out_specs=vmem,
        scratch_shapes=[
            pltpu.VMEM((n, tokens, width_in), bf16),
            pltpu.VMEM((n, tokens, rows_out), bf16),
            pltpu.VMEM(query_grads.shape, bf16),
            pltpu.VMEM(eigenvalues.shape, f32),
            pltpu.VMEM((rows_out // block, block, block), bf16),
            pltpu.VMEM(in_basis.shape, bf16),
            pltpu.VMEM((rows_out // block, block, block), bf16),
            pltpu.VMEM((queries * rows_out, width_in), bf16),
            pltpu.VMEM((CORES * tokens, width_in), bf16),
            pltpu.VMEM((CORES * tokens, rows_out), f32),
            pltpu.VMEM((n // CORES, CORES * tokens, queries * rows_out), f32),
            pltpu.VMEM((8, LANES), f32),
            pltpu.VMEM((n, 1, LANES), f32),
            pltpu.VMEM((n, queries, LANES), f32),
            pltpu.VMEM((8, LANES), f32),
            pltpu.SemaphoreType.DMA((6,)),
            pltpu.SemaphoreType.DMA((n * PARTS, 4)),
            pltpu.SemaphoreType.DMA((n * PARTS,)),
            pltpu.SemaphoreType.DMA,
            pltpu.SemaphoreType.DMA((n,)),
        ] + [pltpu.SemaphoreType.DMA] * 4 + [pltpu.SemaphoreType.REGULAR] * 3,
        compiler_params=pltpu.CompilerParams(
            collective_id=0, has_side_effects=True, vmem_limit_bytes=55040 * 1024
        ),
    )(layer_inputs, output_grads, query_grads, eigenvalues, out_basis, in_basis, doc_lengths[None])


def local(n, *arrays):
    layer_inputs, output_grads, query_grads, _, _, _, doc_lengths = arrays
    tiles, queries, rows_out, rows_in = query_grads.shape
    whole_rows = tiles * rows_in == layer_inputs.shape[1] and n * rows_out == output_grads.shape[1]
    fits = n * layer_inputs.size <= 8 * query_grads.size and doc_lengths.shape[0] <= LANES
    shaped = n % (CORES * ROWS) == 0 and doc_lengths.shape[0] % n == 0 and queries <= 8
    shaped = shaped and layer_inputs.shape[0] % (16 * PARTS) == 0 and n > CORES * ROWS
    if whole_rows and fits and shaped:
        return fused(n, *arrays)
    return tiles_apart(*arrays)


def solution(mesh):
    in_specs = (
        P(("groups", "dp"), None),
        P(("groups", "dp"), None),
        P("dp", None, None, None),
        P("dp", None, None),
        P(),
        P(),
        P("groups"),
    )
    out_specs = P(("groups", "dp"), None)
    return jax.shard_map(functools.partial(local, mesh.shape["dp"]), mesh=mesh, in_specs=in_specs, out_specs=out_specs, check_vma=False)
```

```python
import functools
import math

import jax
import jax.numpy as jnp
from jax import lax
from jax.experimental import pallas as pl
from jax.experimental.pallas import tpu as pltpu
from jax.sharding import PartitionSpec as P


def turn_rows(columns, basis_blocks):
    group_count = basis_blocks.shape[0]
    block_width = basis_blocks.shape[1]
    grouped = columns.reshape(columns.shape[0], group_count, block_width)
    turned = jnp.einsum("tnk,nkj->tnj", grouped, basis_blocks, preferred_element_type=jnp.float32)
    return turned.reshape(columns.shape).astype(jnp.bfloat16)


def precondition(query_grads, eigenvalues, damping, tile_out, tile_in):
    blocks, queries, rows_out, rows_in = query_grads.shape
    block_width = tile_in.shape[-1]
    grouped = query_grads.reshape(blocks, queries, rows_out, rows_in // block_width, block_width)
    half_turned = jnp.einsum(
        "bqonk,bnkj->bqonj", grouped, tile_in, preferred_element_type=jnp.float32
    )
    half_turned = half_turned.reshape(blocks, queries, rows_out, rows_in).astype(jnp.bfloat16)
    grouped = half_turned.reshape(blocks, queries, rows_out // block_width, block_width, rows_in)
    turned = jnp.einsum("bqnki,bnkj->bqnji", grouped, tile_out, preferred_element_type=jnp.float32)
    turned = turned.reshape(blocks, queries, rows_out, rows_in)
    return (turned / (eigenvalues[:, None] + damping)).astype(jnp.bfloat16)


def tally_scores(grads_got, inputs_got, preconditioned, doc_starts, doc_ends):
    blocks, total_rows, rows_out = grads_got.shape
    queries = preconditioned.shape[1]
    row_step = math.gcd(1024, total_rows)
    flat_pre = preconditioned.reshape(blocks, queries * rows_out, preconditioned.shape[3])

    def one_piece(running, piece_index):
        start_row = piece_index * row_step
        grads_piece = lax.dynamic_slice_in_dim(grads_got, start_row, row_step, 1)
        inputs_piece = lax.dynamic_slice_in_dim(inputs_got, start_row, row_step, 1)
        projected = jnp.einsum(
            "bti,bpi->btp", inputs_piece, flat_pre, preferred_element_type=jnp.float32
        )
        projected = projected.reshape(blocks, row_step, queries, rows_out)
        scores = jnp.sum(projected * grads_piece[:, :, None, :].astype(jnp.float32), axis=(0, 3))
        positions = start_row + lax.iota(jnp.int32, row_step)
        member = (
            (positions[:, None] >= doc_starts[None, :]) & (positions[:, None] < doc_ends[None, :])
        ).astype(jnp.float32)
        added = jnp.einsum("td,tq->dq", member, scores, precision=lax.Precision.HIGHEST)
        return (running + added, None)

    initial = jnp.zeros((doc_starts.shape[0], queries), jnp.float32)
    summed, _ = lax.scan(one_piece, initial, jnp.arange(total_rows // row_step, dtype=jnp.int32))
    return summed


def tiles_apart(layer_inputs, output_grads, query_grads, eigenvalues, out_basis, in_basis, doc_lengths):
    block_width = out_basis.shape[1]
    tok_count = layer_inputs.shape[0]
    tile_count = query_grads.shape[0]
    rows_out = query_grads.shape[2]
    rows_in = query_grads.shape[3]
    in_tiles = layer_inputs.shape[1] // rows_in
    out_tiles = output_grads.shape[1] // rows_out
    tile_ids = lax.axis_index("dp") * tile_count + lax.iota(jnp.int32, tile_count)
    out_sets = out_basis.reshape(out_tiles, rows_out // block_width, block_width, block_width)
    in_sets = in_basis.reshape(in_tiles, rows_in // block_width, block_width, block_width)
    tile_out = jnp.take(out_sets, tile_ids // in_tiles, axis=0)
    tile_in = jnp.take(in_sets, tile_ids % in_tiles, axis=0)
    eigen_sum = lax.psum(jnp.sum(eigenvalues), "dp")
    entries = output_grads.shape[1] * layer_inputs.shape[1]
    damping = 0.1 * (eigen_sum / entries)
    preconditioned = precondition(query_grads, eigenvalues, damping, tile_out, tile_in)
    grads_local = turn_rows(output_grads, out_basis)
    inputs_local = turn_rows(layer_inputs, in_basis)
    grads_tiles = grads_local.reshape(tok_count, out_tiles, rows_out).transpose(1, 0, 2)[:, None]
    grads_tiles = jnp.broadcast_to(grads_tiles, (out_tiles, in_tiles, tok_count, rows_out))
    grads_tiles = grads_tiles.reshape(out_tiles * in_tiles, tok_count, rows_out)
    inputs_tiles = inputs_local.reshape(tok_count, in_tiles, rows_in).transpose(1, 0, 2)[None]
    inputs_tiles = jnp.broadcast_to(inputs_tiles, (out_tiles, in_tiles, tok_count, rows_in))
    inputs_tiles = inputs_tiles.reshape(out_tiles * in_tiles, tok_count, rows_in)
    grads_got, inputs_got = (
        lax.all_to_all(grads_tiles, "dp", split_axis=0, concat_axis=1, tiled=True),
        lax.all_to_all(inputs_tiles, "dp", split_axis=0, concat_axis=1, tiled=True),
    )
    doc_ends = jnp.cumsum(doc_lengths)
    doc_starts = doc_ends - doc_lengths
    partial_scores = tally_scores(grads_got, inputs_got, preconditioned, doc_starts, doc_ends)
    return lax.psum_scatter(partial_scores, "dp", scatter_dimension=0, tiled=True)


CORES = 2
ROWS = 2
PARTS = 2
LANES = 128
MESH = pl.DeviceIdType.MESH


def fused_kernel(
    n, eigen_count,
    x_ref, y_ref, query_ref, eigen_ref, outb_ref, inb_ref, lengths_ref,
    out_ref,
    x_all, y_all, query, eigen, outb, inb, outb_t, pre, rotated, grads_rot, projected, counts, lengths, e_buf, f_buf, acc,
    local_sem, x_send, x_recv, y_send, y_recv, e_send, e_recv, f_send, f_recv, plane_in, below_in, above_in,
):
    planes = n // (CORES * ROWS)
    group, me = lax.axis_index("groups"), lax.axis_index("dp")
    core = lax.rem(me, CORES)
    row = lax.rem(me // CORES, ROWS)
    plane = me // (CORES * ROWS)
    tokens, width_in = x_ref.shape
    width_out = y_all.shape[2]
    tiles, queries, rows_out, rows_in = query_ref.shape
    block = outb_ref.shape[1]
    out_blocks = rows_out // block
    in_blocks = width_in // block
    blocks_per_tile = rows_in // block

    def slot_of(p, r, c):
        return (p * ROWS + r) * CORES + c

    up, down = me + CORES * ROWS, me - CORES * ROWS
    across = slot_of(plane, 1 - row, core)
    partner = slot_of(plane, row, 1 - core)
    has_up, has_down = plane < planes - 1, plane > 0
    at_end = (plane == 0) | (plane == planes - 1)

    def x_copy(src, slot, channel, target, part):
        span = pl.ds(part * (tokens // PARTS), tokens // PARTS)
        return pltpu.make_async_remote_copy(
            src_ref=src.at[span], dst_ref=x_all.at[slot, span],
            send_sem=x_send.at[slot * PARTS + part, channel],
            recv_sem=x_recv.at[slot * PARTS + part],
            device_id=(group, target), device_id_type=MESH,
        )

    def x_arrived(slot, part):
        x_copy(x_all.at[slot], slot, 0, across, part).wait_recv()

    def x_forward(slot, channel, target, part):
        x_copy(x_all.at[slot], slot, channel, target, part).start()

    def y_copy(target):
        columns = pl.ds(pl.multiple_of(target * width_out, width_out), width_out)
        return pltpu.make_async_remote_copy(
            src_ref=y_ref.at[:, columns], dst_ref=y_all.at[me],
            send_sem=y_send, recv_sem=y_recv.at[me],
            device_id=(group, target), device_id_type=MESH,
        )

    def y_arrived(source):
        pltpu.make_async_remote_copy(
            src_ref=y_all.at[source], dst_ref=y_all.at[source],
            send_sem=y_send, recv_sem=y_recv.at[source],
            device_id=(group, across), device_id_type=MESH,
        ).wait_recv()

    def small_copy(buf, send, recv, source, target):
        return pltpu.make_async_remote_copy(
            src_ref=buf.at[source], dst_ref=buf.at[source],
            send_sem=send, recv_sem=recv,
            device_id=(group, target), device_id_type=MESH,
        )

    def all_sent(buf, send):
        every = buf.at[pl.ds(0, n - 1)]
        pltpu.make_async_copy(every, every, send).wait()

    def loop(low, high, body):
        def step(j, carry):
            body(j)
            return carry
        lax.fori_loop(low, high, step, 0)

    def others(body):
        loop(1, n, lambda j: body(lax.rem(me + j, n)))

    def y_send_row(p, r):
        loop(0, CORES, lambda j: y_copy(slot_of(p, r, lax.rem(core + j, CORES))).start())

    def y_send_planes(count, plane_at):
        def one(j):
            y_send_row(plane_at(j // ROWS), lax.rem(row + j, ROWS))
        loop(0, ROWS * count, one)

    def sides(k, body):
        def one(side):
            p = plane + k * (2 * side - 1)
            @pl.when((p >= 0) & (p < planes))
            def _():
                body(p)
        loop(0, 2, one)

    def from_across(p):
        slot = slot_of(p, 1 - row, core)
        for part in range(PARTS):
            x_arrived(slot, part)
            x_forward(slot, 3, partner, part)

    def from_line(p):
        slot = slot_of(p, row, core)
        for part in range(PARTS):
            x_arrived(slot, part)

            @pl.when((p < plane) & has_up)
            def _():
                x_forward(slot, 0, up, part)

            @pl.when((p > plane) & has_down)
            def _():
                x_forward(slot, 1, down, part)

            x_forward(slot, 2, across, part)
            x_forward(slot, 3, partner, part)

    def lines(k):
        sides(k, from_line)

        @pl.when((plane == k) & has_up)
        def _():
            y_send_planes(planes - 1 - plane, lambda j: plane + 1 + j)

        @pl.when((planes - 1 - plane == k) & has_down)
        def _():
            y_send_planes(plane, lambda j: plane - 1 - j)

    own_columns = pl.ds(pl.multiple_of(me * width_out, width_out), width_out)
    own_out = pl.ds(me * out_blocks, out_blocks)
    loads = [
        pltpu.make_async_copy(eigen_ref, eigen, local_sem.at[0]),
        pltpu.make_async_copy(query_ref, query, local_sem.at[1]),
        pltpu.make_async_copy(outb_ref.at[own_out], outb, local_sem.at[2]),
        pltpu.make_async_copy(inb_ref, inb, local_sem.at[3]),
        pltpu.make_async_copy(x_ref, x_all.at[me], local_sem.at[4]),
        pltpu.make_async_copy(y_ref.at[:, own_columns], y_all.at[me], local_sem.at[5]),
        pltpu.make_async_copy(lengths_ref, counts, local_sem.at[6]),
    ]

    barrier = pltpu.get_barrier_semaphore()

    def greet(semaphore, target):
        pl.semaphore_signal(semaphore, inc=1, device_id=(group, target), device_id_type=MESH)

    @pl.when(has_up)
    def _():
        greet(barrier, up)

    @pl.when(has_down)
    def _():
        greet(barrier, down)

    greet(barrier, across)
    greet(barrier, partner)
    for load in loads:
        load.start()
    pl.semaphore_wait(barrier, 2 + has_up.astype(jnp.int32) + has_down.astype(jnp.int32))

    for part in range(PARTS):
        @pl.when(has_up)
        def _():
            x_copy(x_ref, me, 0, up, part).start()

        @pl.when(has_down)
        def _():
            x_copy(x_ref, me, 1, down, part).start()

        x_copy(x_ref, me, 2, across, part).start()
        x_copy(x_ref, me, 3, partner, part).start()

    greet(plane_in, partner)
    pl.semaphore_wait(plane_in, 1)

    @pl.when(plane == 0)
    def _():
        greet(below_in, up)

    @pl.when(plane == planes - 1)
    def _():
        greet(above_in, down)

    loads[0].wait()

    def add_tile(b, carry):
        tile = eigen[b]
        folded = tile[:, :LANES]
        for lane in range(LANES, rows_in, LANES):
            folded = folded + tile[:, lane:lane + LANES]
        return carry + jnp.sum(folded.reshape(rows_out // 8, 8, LANES), axis=0)

    eigen_total = lax.fori_loop(0, tiles, add_tile, jnp.zeros((8, LANES), jnp.float32))
    e_buf[me] = jnp.sum(eigen_total, axis=0, keepdims=True)

    @pl.when(has_down)
    def _():
        pl.semaphore_wait(below_in, 1)

        @pl.when(has_up)
        def _():
            greet(below_in, up)

    @pl.when(has_up)
    def _():
        pl.semaphore_wait(above_in, 1)

        @pl.when(has_down)
        def _():
            greet(above_in, down)

    others(lambda t: small_copy(e_buf, e_send, e_recv, me, t).start())

    @pl.when(at_end)
    def _():
        def outward(j):
            k = j + 1
            return jnp.where(plane == 0, k, planes - 1 - k)
        y_send_planes(planes - 1, outward)

    for load in loads[1:4]:
        load.wait()
    for j in range(out_blocks):
        outb_t[j] = outb[j].astype(jnp.float32).T.astype(jnp.bfloat16)

    def half_turn(b):
        for q in range(queries):
            for k in range(blocks_per_tile):
                lanes = slice(k * block, (k + 1) * block)
                query[b, q, :, lanes] = jnp.dot(
                    query[b, q, :, lanes], inb[b * blocks_per_tile + k],
                    preferred_element_type=jnp.float32,
                ).astype(jnp.bfloat16)

    loop(0, tiles, half_turn)
    lines(1)
    all_sent(e_buf, e_recv)
    damping = 0.1 * (jnp.sum(e_buf[...]) / eigen_count)

    def finish(b):
        columns = pl.ds(pl.multiple_of(b * rows_in, rows_in), rows_in)
        for j in range(out_blocks):
            span = slice(j * block, (j + 1) * block)
            inverse = 1.0 / (eigen[b, span, :] + damping)
            for q in range(queries):
                turned = jnp.dot(outb_t[j], query[b, q, span, :], preferred_element_type=jnp.float32)
                pre[q * rows_out + j * block:q * rows_out + (j + 1) * block, columns] = (
                    turned * inverse
                ).astype(jnp.bfloat16)

    loop(0, tiles, finish)
    for load in loads[4:]:
        load.wait()
    acc[...] = jnp.zeros_like(acc)
    lanes_of_docs = acc.shape[1]
    rows = CORES * tokens
    docs = lengths_ref.shape[1]
    lengths[...] = jnp.zeros_like(lengths)
    lengths[0:1, 0:docs] = counts[...].astype(jnp.float32)
    lengths_row = lengths[0:1, :]
    lengths_down = jnp.broadcast_to(lengths_row, (lanes_of_docs, lanes_of_docs)).T
    earlier = lax.broadcasted_iota(jnp.int32, lengths_down.shape, 0)
    earlier = earlier <= lax.broadcasted_iota(jnp.int32, lengths_down.shape, 1)
    ends = jnp.sum(jnp.where(earlier, lengths_down, 0.0), axis=0, keepdims=True)
    lengths[1:2, :] = ends
    lengths[0:1, :] = ends - lengths_row

    def project_chip(p, r):
        base = slot_of(p, r, 0)
        for part in range(PARTS):
            x_arrived(base + 1 - core, part)
        for c in range(CORES):
            spot = slice(c * tokens, (c + 1) * tokens)
            for k in range(in_blocks):
                lanes = slice(k * block, (k + 1) * block)
                rotated[spot, lanes] = jnp.dot(
                    x_all[base + c, :, lanes], inb[k], preferred_element_type=jnp.float32
                ).astype(jnp.bfloat16)
        step = math.gcd(queries * rows_out, 256)
        for o in range(0, queries * rows_out, step):
            projected[p * ROWS + r, :, o:o + step] = lax.dot_general(
                rotated[...], pre[o:o + step, :], (((1,), (1,)), ((), ())),
                preferred_element_type=jnp.float32,
            )

    def tally_chip(p, r):
        base = slot_of(p, r, 0)
        for c in range(CORES):
            @pl.when(base + c != me)
            def _():
                y_arrived(base + c)
        for c in range(CORES):
            spot = slice(c * tokens, (c + 1) * tokens)
            for k in range(out_blocks):
                lanes = slice(k * block, (k + 1) * block)
                grads_rot[spot, lanes] = jnp.dot(
                    y_all[base + c, :, lanes], outb[k], preferred_element_type=jnp.float32
                ).astype(jnp.bfloat16).astype(jnp.float32)
        positions = base * tokens + lax.broadcasted_iota(jnp.int32, (rows, lanes_of_docs), 0)
        positions = positions.astype(jnp.float32)
        member = (positions >= lengths[0:1, :]) & (positions < lengths[1:2, :])
        for q in range(queries):
            total = jnp.zeros((rows, LANES), jnp.float32)
            for lane in range(0, rows_out, LANES):
                total = total + (
                    projected[p * ROWS + r, :, q * rows_out + lane:q * rows_out + lane + LANES]
                    * grads_rot[:, lane:lane + LANES]
                )
            score = jnp.sum(total, axis=1, keepdims=True)
            added = jnp.sum(jnp.where(member, score, 0.0), axis=0, keepdims=True)
            acc[q:q + 1, :] = acc[q:q + 1, :] + added

    def project_plane(p):
        from_across(p)
        loop(0, ROWS, lambda r: project_chip(p, lax.rem(row + r, ROWS)))

    project_plane(plane)
    loop(2, planes, lines)

    y_copy(partner).start()
    y_copy(across).start()
    y_copy(slot_of(plane, 1 - row, 1 - core)).start()
    loop(1, planes, lambda k: sides(k, project_plane))
    turn = jnp.where(2 * plane < planes, planes - 1, 1)

    def tally_plane(j):
        p = lax.rem(plane + turn * j, planes)
        loop(0, ROWS, lambda r: tally_chip(p, lax.rem(row + r, ROWS)))

    loop(0, planes - 1, tally_plane)
    def left(slot, channel):
        for part in range(PARTS):
            x_copy(x_all.at[slot], slot, channel, across, part).wait_send()

    def drain(p):
        slot = slot_of(p, row, core)

        @pl.when((p <= plane) & has_up)
        def _():
            left(slot, 0)

        @pl.when((p >= plane) & has_down)
        def _():
            left(slot, 1)

        left(slot, 2)
        left(slot, 3)
        left(slot_of(p, 1 - row, core), 3)

    loop(0, planes, drain)
    loop(planes - 1, planes, tally_plane)
    f_buf[me] = acc[0:queries, :]
    others(lambda t: small_copy(f_buf, f_send, f_recv, me, t).start())

    all_sent(y_all, y_send)
    all_sent(e_buf, e_send)
    all_sent(f_buf, f_recv)
    all_sent(f_buf, f_send)
    summed = jnp.sum(f_buf[...], axis=0)
    lane = lax.broadcasted_iota(jnp.int32, summed.shape, 1)
    per_device = out_ref.shape[0]
    for j in range(per_device):
        picked = jnp.sum(jnp.where(lane == me * per_device + j, summed, 0.0), axis=1, keepdims=True)
        for q in range(queries):
            out_ref[j:j + 1, q:q + 1] = picked[q:q + 1, :]


def fused(n, layer_inputs, output_grads, query_grads, eigenvalues, out_basis, in_basis, doc_lengths):
    tokens, width_in = layer_inputs.shape
    tiles, queries, rows_out, rows_in = query_grads.shape
    docs = doc_lengths.shape[0]
    block = out_basis.shape[1]
    anyspace = pl.BlockSpec(memory_space=pl.ANY)
    vmem = pl.BlockSpec(memory_space=pltpu.VMEM)
    bf16, f32 = jnp.bfloat16, jnp.float32
    return pl.pallas_call(
        functools.partial(fused_kernel, n, output_grads.shape[1] * width_in),
        out_shape=jax.ShapeDtypeStruct((docs // n, queries), f32),
        in_specs=[anyspace] * 6 + [pl.BlockSpec(memory_space=pltpu.HBM)],
        out_specs=vmem,
        scratch_shapes=[
            pltpu.VMEM((n, tokens, width_in), bf16),
            pltpu.VMEM((n, tokens, rows_out), bf16),
            pltpu.VMEM(query_grads.shape, bf16),
            pltpu.VMEM(eigenvalues.shape, f32),
            pltpu.VMEM((rows_out // block, block, block), bf16),
            pltpu.VMEM(in_basis.shape, bf16),
            pltpu.VMEM((rows_out // block, block, block), bf16),
            pltpu.VMEM((queries * rows_out, width_in), bf16),
            pltpu.VMEM((CORES * tokens, width_in), bf16),
            pltpu.VMEM((CORES * tokens, rows_out), f32),
            pltpu.VMEM((n // CORES, CORES * tokens, queries * rows_out), f32),
            pltpu.VMEM((1, docs), jnp.int32),
            pltpu.VMEM((8, LANES), f32),
            pltpu.VMEM((n, 1, LANES), f32),
            pltpu.VMEM((n, queries, LANES), f32),
            pltpu.VMEM((8, LANES), f32),
            pltpu.SemaphoreType.DMA((7,)),
            pltpu.SemaphoreType.DMA((n * PARTS, 4)),
            pltpu.SemaphoreType.DMA((n * PARTS,)),
            pltpu.SemaphoreType.DMA,
            pltpu.SemaphoreType.DMA((n,)),
        ] + [pltpu.SemaphoreType.DMA] * 4 + [pltpu.SemaphoreType.REGULAR] * 3,
        compiler_params=pltpu.CompilerParams(
            collective_id=0, has_side_effects=True, vmem_limit_bytes=55040 * 1024
        ),
    )(layer_inputs, output_grads, query_grads, eigenvalues, out_basis, in_basis, doc_lengths[None])


def local(n, *arrays):
    layer_inputs, output_grads, query_grads, _, _, _, doc_lengths = arrays
    tiles, queries, rows_out, rows_in = query_grads.shape
    whole_rows = tiles * rows_in == layer_inputs.shape[1] and n * rows_out == output_grads.shape[1]
    fits = n * layer_inputs.size <= 8 * query_grads.size and doc_lengths.shape[0] <= LANES
    shaped = n % (CORES * ROWS) == 0 and doc_lengths.shape[0] % n == 0 and queries <= 8
    shaped = shaped and layer_inputs.shape[0] % (16 * PARTS) == 0 and n > CORES * ROWS
    if whole_rows and fits and shaped:
        return fused(n, *arrays)
    return tiles_apart(*arrays)


def solution(mesh):
    in_specs = (
        P(("groups", "dp"), None),
        P(("groups", "dp"), None),
        P("dp", None, None, None),
        P("dp", None, None),
        P(),
        P(),
        P("groups"),
    )
    out_specs = P(("groups", "dp"), None)
    return jax.shard_map(functools.partial(local, mesh.shape["dp"]), mesh=mesh, in_specs=in_specs, out_specs=out_specs, check_vma=False)
```

```python
import functools
import math

import jax
import jax.numpy as jnp
from jax import lax
from jax.experimental import pallas as pl
from jax.experimental.pallas import tpu as pltpu
from jax.sharding import PartitionSpec as P


def turn_rows(columns, basis_blocks):
    group_count = basis_blocks.shape[0]
    block_width = basis_blocks.shape[1]
    grouped = columns.reshape(columns.shape[0], group_count, block_width)
    turned = jnp.einsum("tnk,nkj->tnj", grouped, basis_blocks, preferred_element_type=jnp.float32)
    return turned.reshape(columns.shape).astype(jnp.bfloat16)


def precondition(query_grads, eigenvalues, damping, tile_out, tile_in):
    blocks, queries, rows_out, rows_in = query_grads.shape
    block_width = tile_in.shape[-1]
    grouped = query_grads.reshape(blocks, queries, rows_out, rows_in // block_width, block_width)
    half_turned = jnp.einsum(
        "bqonk,bnkj->bqonj", grouped, tile_in, preferred_element_type=jnp.float32
    )
    half_turned = half_turned.reshape(blocks, queries, rows_out, rows_in).astype(jnp.bfloat16)
    grouped = half_turned.reshape(blocks, queries, rows_out // block_width, block_width, rows_in)
    turned = jnp.einsum("bqnki,bnkj->bqnji", grouped, tile_out, preferred_element_type=jnp.float32)
    turned = turned.reshape(blocks, queries, rows_out, rows_in)
    return (turned / (eigenvalues[:, None] + damping)).astype(jnp.bfloat16)


def tally_scores(grads_got, inputs_got, preconditioned, doc_starts, doc_ends):
    blocks, total_rows, rows_out = grads_got.shape
    queries = preconditioned.shape[1]
    row_step = math.gcd(1024, total_rows)
    flat_pre = preconditioned.reshape(blocks, queries * rows_out, preconditioned.shape[3])

    def one_piece(running, piece_index):
        start_row = piece_index * row_step
        grads_piece = lax.dynamic_slice_in_dim(grads_got, start_row, row_step, 1)
        inputs_piece = lax.dynamic_slice_in_dim(inputs_got, start_row, row_step, 1)
        projected = jnp.einsum(
            "bti,bpi->btp", inputs_piece, flat_pre, preferred_element_type=jnp.float32
        )
        projected = projected.reshape(blocks, row_step, queries, rows_out)
        scores = jnp.sum(projected * grads_piece[:, :, None, :].astype(jnp.float32), axis=(0, 3))
        positions = start_row + lax.iota(jnp.int32, row_step)
        member = (
            (positions[:, None] >= doc_starts[None, :]) & (positions[:, None] < doc_ends[None, :])
        ).astype(jnp.float32)
        added = jnp.einsum("td,tq->dq", member, scores, precision=lax.Precision.HIGHEST)
        return (running + added, None)

    initial = jnp.zeros((doc_starts.shape[0], queries), jnp.float32)
    summed, _ = lax.scan(one_piece, initial, jnp.arange(total_rows // row_step, dtype=jnp.int32))
    return summed


def tiles_apart(layer_inputs, output_grads, query_grads, eigenvalues, out_basis, in_basis, doc_lengths):
    block_width = out_basis.shape[1]
    tok_count = layer_inputs.shape[0]
    tile_count = query_grads.shape[0]
    rows_out = query_grads.shape[2]
    rows_in = query_grads.shape[3]
    in_tiles = layer_inputs.shape[1] // rows_in
    out_tiles = output_grads.shape[1] // rows_out
    tile_ids = lax.axis_index("dp") * tile_count + lax.iota(jnp.int32, tile_count)
    out_sets = out_basis.reshape(out_tiles, rows_out // block_width, block_width, block_width)
    in_sets = in_basis.reshape(in_tiles, rows_in // block_width, block_width, block_width)
    tile_out = jnp.take(out_sets, tile_ids // in_tiles, axis=0)
    tile_in = jnp.take(in_sets, tile_ids % in_tiles, axis=0)
    eigen_sum = lax.psum(jnp.sum(eigenvalues), "dp")
    entries = output_grads.shape[1] * layer_inputs.shape[1]
    damping = 0.1 * (eigen_sum / entries)
    preconditioned = precondition(query_grads, eigenvalues, damping, tile_out, tile_in)
    grads_local = turn_rows(output_grads, out_basis)
    inputs_local = turn_rows(layer_inputs, in_basis)
    grads_tiles = grads_local.reshape(tok_count, out_tiles, rows_out).transpose(1, 0, 2)[:, None]
    grads_tiles = jnp.broadcast_to(grads_tiles, (out_tiles, in_tiles, tok_count, rows_out))
    grads_tiles = grads_tiles.reshape(out_tiles * in_tiles, tok_count, rows_out)
    inputs_tiles = inputs_local.reshape(tok_count, in_tiles, rows_in).transpose(1, 0, 2)[None]
    inputs_tiles = jnp.broadcast_to(inputs_tiles, (out_tiles, in_tiles, tok_count, rows_in))
    inputs_tiles = inputs_tiles.reshape(out_tiles * in_tiles, tok_count, rows_in)
    grads_got, inputs_got = (
        lax.all_to_all(grads_tiles, "dp", split_axis=0, concat_axis=1, tiled=True),
        lax.all_to_all(inputs_tiles, "dp", split_axis=0, concat_axis=1, tiled=True),
    )
    doc_ends = jnp.cumsum(doc_lengths)
    doc_starts = doc_ends - doc_lengths
    partial_scores = tally_scores(grads_got, inputs_got, preconditioned, doc_starts, doc_ends)
    return lax.psum_scatter(partial_scores, "dp", scatter_dimension=0, tiled=True)


CORES = 2
ROWS = 2
PARTS = 2
LANES = 128
MESH = pl.DeviceIdType.MESH


def fused_kernel(
    n, eigen_count,
    x_ref, y_ref, query_ref, eigen_ref, outb_ref, inb_ref, lengths_ref,
    out_ref,
    x_all, y_all, query, eigen, outb, inb, outb_t, pre, rotated, grads_rot, projected, lengths, e_buf, f_buf, acc,
    local_sem, x_send, x_recv, y_send, y_recv, e_send, e_recv, f_send, f_recv, plane_in, below_in, above_in,
):
    planes = n // (CORES * ROWS)
    group, me = lax.axis_index("groups"), lax.axis_index("dp")
    core = lax.rem(me, CORES)
    row = lax.rem(me // CORES, ROWS)
    plane = me // (CORES * ROWS)
    tokens, width_in = x_ref.shape
    width_out = y_all.shape[2]
    tiles, queries, rows_out, rows_in = query_ref.shape
    block = outb_ref.shape[1]
    out_blocks = rows_out // block
    in_blocks = width_in // block
    blocks_per_tile = rows_in // block

    def slot_of(p, r, c):
        return (p * ROWS + r) * CORES + c

    up, down = me + CORES * ROWS, me - CORES * ROWS
    across = slot_of(plane, 1 - row, core)
    partner = slot_of(plane, row, 1 - core)
    has_up, has_down = plane < planes - 1, plane > 0
    at_end = (plane == 0) | (plane == planes - 1)

    def x_copy(src, slot, channel, target, part):
        span = pl.ds(part * (tokens // PARTS), tokens // PARTS)
        return pltpu.make_async_remote_copy(
            src_ref=src.at[span], dst_ref=x_all.at[slot, span],
            send_sem=x_send.at[slot * PARTS + part, channel],
            recv_sem=x_recv.at[slot * PARTS + part],
            device_id=(group, target), device_id_type=MESH,
        )

    def x_arrived(slot, part):
        x_copy(x_all.at[slot], slot, 0, across, part).wait_recv()

    def x_forward(slot, channel, target, part):
        x_copy(x_all.at[slot], slot, channel, target, part).start()

    def y_copy(target):
        columns = pl.ds(pl.multiple_of(target * width_out, width_out), width_out)
        return pltpu.make_async_remote_copy(
            src_ref=y_ref.at[:, columns], dst_ref=y_all.at[me],
            send_sem=y_send, recv_sem=y_recv.at[me],
            device_id=(group, target), device_id_type=MESH,
        )

    def y_arrived(source):
        pltpu.make_async_remote_copy(
            src_ref=y_all.at[source], dst_ref=y_all.at[source],
            send_sem=y_send, recv_sem=y_recv.at[source],
            device_id=(group, across), device_id_type=MESH,
        ).wait_recv()

    def small_copy(buf, send, recv, source, target):
        return pltpu.make_async_remote_copy(
            src_ref=buf.at[source], dst_ref=buf.at[source],
            send_sem=send, recv_sem=recv,
            device_id=(group, target), device_id_type=MESH,
        )

    def all_sent(buf, send):
        every = buf.at[pl.ds(0, n - 1)]
        pltpu.make_async_copy(every, every, send).wait()

    def loop(low, high, body):
        def step(j, carry):
            body(j)
            return carry
        lax.fori_loop(low, high, step, 0)

    def others(body):
        loop(0, n - 1, lambda j: body(lax.rem(me + 1 + lax.rem(j + n // 2 - 1, n - 1), n)))

    def y_send_row(p, r):
        loop(0, CORES, lambda j: y_copy(slot_of(p, r, lax.rem(core + j, CORES))).start())

    def y_send_planes(count, plane_at):
        def one(j):
            y_send_row(plane_at(j // ROWS), lax.rem(row + j, ROWS))
        loop(0, ROWS * count, one)

    def sides(k, body):
        def one(side):
            p = plane + k * (2 * side - 1)
            @pl.when((p >= 0) & (p < planes))
            def _():
                body(p)
        loop(0, 2, one)

    def from_across(p):
        slot = slot_of(p, 1 - row, core)
        for part in range(PARTS):
            x_arrived(slot, part)
            x_forward(slot, 3, partner, part)

    def from_line(p):
        slot = slot_of(p, row, core)
        for part in range(PARTS):
            x_arrived(slot, part)

            @pl.when((p < plane) & has_up)
            def _():
                x_forward(slot, 0, up, part)

            @pl.when((p > plane) & has_down)
            def _():
                x_forward(slot, 1, down, part)

            x_forward(slot, 2, across, part)
            x_forward(slot, 3, partner, part)

    def lines(k):
        sides(k, from_line)

        @pl.when((plane == k) & has_up)
        def _():
            y_send_planes(planes - 1 - plane, lambda j: plane + 1 + j)

        @pl.when((planes - 1 - plane == k) & has_down)
        def _():
            y_send_planes(plane, lambda j: plane - 1 - j)

    own_columns = pl.ds(pl.multiple_of(me * width_out, width_out), width_out)
    own_out = pl.ds(me * out_blocks, out_blocks)
    loads = [
        pltpu.make_async_copy(eigen_ref, eigen, local_sem.at[0]),
        pltpu.make_async_copy(query_ref, query, local_sem.at[1]),
        pltpu.make_async_copy(outb_ref.at[own_out], outb, local_sem.at[2]),
        pltpu.make_async_copy(inb_ref, inb, local_sem.at[3]),
        pltpu.make_async_copy(x_ref, x_all.at[me], local_sem.at[4]),
        pltpu.make_async_copy(y_ref.at[:, own_columns], y_all.at[me], local_sem.at[5]),
    ]

    barrier = pltpu.get_barrier_semaphore()

    def greet(semaphore, target):
        pl.semaphore_signal(semaphore, inc=1, device_id=(group, target), device_id_type=MESH)

    @pl.when(has_up)
    def _():
        greet(barrier, up)

    @pl.when(has_down)
    def _():
        greet(barrier, down)

    greet(barrier, across)
    greet(barrier, partner)
    for load in loads:
        load.start()
    pl.semaphore_wait(barrier, 2 + has_up.astype(jnp.int32) + has_down.astype(jnp.int32))

    for part in range(PARTS):
        @pl.when(has_up)
        def _():
            x_copy(x_ref, me, 0, up, part).start()

        @pl.when(has_down)
        def _():
            x_copy(x_ref, me, 1, down, part).start()

        x_copy(x_ref, me, 2, across, part).start()
        x_copy(x_ref, me, 3, partner, part).start()

    greet(plane_in, partner)
    pl.semaphore_wait(plane_in, 1)

    @pl.when(plane == 0)
    def _():
        greet(below_in, up)

    @pl.when(plane == planes - 1)
    def _():
        greet(above_in, down)

    loads[0].wait()

    def add_tile(b, carry):
        tile = eigen[b]
        folded = tile[:, :LANES]
        for lane in range(LANES, rows_in, LANES):
            folded = folded + tile[:, lane:lane + LANES]
        return carry + jnp.sum(folded.reshape(rows_out // 8, 8, LANES), axis=0)

    eigen_total = lax.fori_loop(0, tiles, add_tile, jnp.zeros((8, LANES), jnp.float32))
    e_buf[me] = jnp.sum(eigen_total, axis=0, keepdims=True)

    @pl.when(has_down)
    def _():
        pl.semaphore_wait(below_in, 1)

        @pl.when(has_up)
        def _():
            greet(below_in, up)

    @pl.when(has_up)
    def _():
        pl.semaphore_wait(above_in, 1)

        @pl.when(has_down)
        def _():
            greet(above_in, down)

    others(lambda t: small_copy(e_buf, e_send, e_recv, me, t).start())

    @pl.when(at_end)
    def _():
        def outward(j):
            k = j + 1
            return jnp.where(plane == 0, k, planes - 1 - k)
        y_send_planes(planes - 1, outward)

    for load in loads[1:4]:
        load.wait()
    for j in range(out_blocks):
        outb_t[j] = outb[j].astype(jnp.float32).T.astype(jnp.bfloat16)

    def half_turn(b):
        for q in range(queries):
            for k in range(blocks_per_tile):
                lanes = slice(k * block, (k + 1) * block)
                query[b, q, :, lanes] = jnp.dot(
                    query[b, q, :, lanes], inb[b * blocks_per_tile + k],
                    preferred_element_type=jnp.float32,
                ).astype(jnp.bfloat16)

    loop(0, tiles, half_turn)
    lines(1)
    all_sent(e_buf, e_recv)
    damping = 0.1 * (jnp.sum(e_buf[...]) / eigen_count)

    def finish(b):
        columns = pl.ds(pl.multiple_of(b * rows_in, rows_in), rows_in)
        for j in range(out_blocks):
            span = slice(j * block, (j + 1) * block)
            inverse = 1.0 / (eigen[b, span, :] + damping)
            for q in range(queries):
                turned = jnp.dot(outb_t[j], query[b, q, span, :], preferred_element_type=jnp.float32)
                pre[q * rows_out + j * block:q * rows_out + (j + 1) * block, columns] = (
                    turned * inverse
                ).astype(jnp.bfloat16)

    loop(0, tiles, finish)
    for load in loads[4:]:
        load.wait()
    acc[...] = jnp.zeros_like(acc)
    lanes_of_docs = acc.shape[1]
    rows = CORES * tokens
    docs = lengths_ref.shape[1]
    lengths[...] = jnp.zeros_like(lengths)
    lengths[0:1, 0:docs] = lengths_ref[...].astype(jnp.float32)
    lengths_row = lengths[0:1, :]
    lengths_down = jnp.broadcast_to(lengths_row, (lanes_of_docs, lanes_of_docs)).T
    earlier = lax.broadcasted_iota(jnp.int32, lengths_down.shape, 0)
    earlier = earlier <= lax.broadcasted_iota(jnp.int32, lengths_down.shape, 1)
    ends = jnp.sum(jnp.where(earlier, lengths_down, 0.0), axis=0, keepdims=True)
    lengths[1:2, :] = ends
    lengths[0:1, :] = ends - lengths_row

    def project_chip(p, r):
        base = slot_of(p, r, 0)
        for part in range(PARTS):
            x_arrived(base + 1 - core, part)
        for c in range(CORES):
            spot = slice(c * tokens, (c + 1) * tokens)
            for k in range(in_blocks):
                lanes = slice(k * block, (k + 1) * block)
                rotated[spot, lanes] = jnp.dot(
                    x_all[base + c, :, lanes], inb[k], preferred_element_type=jnp.float32
                ).astype(jnp.bfloat16)
        step = math.gcd(queries * rows_out, 256)
        for o in range(0, queries * rows_out, step):
            projected[p * ROWS + r, :, o:o + step] = lax.dot_general(
                rotated[...], pre[o:o + step, :], (((1,), (1,)), ((), ())),
                preferred_element_type=jnp.float32,
            )

    def tally_chip(p, r):
        base = slot_of(p, r, 0)
        for c in range(CORES):
            @pl.when(base + c != me)
            def _():
                y_arrived(base + c)
        for c in range(CORES):
            spot = slice(c * tokens, (c + 1) * tokens)
            for k in range(out_blocks):
                lanes = slice(k * block, (k + 1) * block)
                grads_rot[spot, lanes] = jnp.dot(
                    y_all[base + c, :, lanes], outb[k], preferred_element_type=jnp.float32
                ).astype(jnp.bfloat16).astype(jnp.float32)
        positions = base * tokens + lax.broadcasted_iota(jnp.int32, (rows, lanes_of_docs), 0)
        positions = positions.astype(jnp.float32)
        member = (positions >= lengths[0:1, :]) & (positions < lengths[1:2, :])
        for q in range(queries):
            total = jnp.zeros((rows, LANES), jnp.float32)
            for lane in range(0, rows_out, LANES):
                total = total + (
                    projected[p * ROWS + r, :, q * rows_out + lane:q * rows_out + lane + LANES]
                    * grads_rot[:, lane:lane + LANES]
                )
            score = jnp.sum(total, axis=1, keepdims=True)
            added = jnp.sum(jnp.where(member, score, 0.0), axis=0, keepdims=True)
            acc[q:q + 1, :] = acc[q:q + 1, :] + added

    def project_plane(p):
        from_across(p)
        loop(0, ROWS, lambda r: project_chip(p, lax.rem(row + r, ROWS)))

    project_plane(plane)
    loop(2, planes, lines)

    y_copy(partner).start()
    y_copy(across).start()
    y_copy(slot_of(plane, 1 - row, 1 - core)).start()
    loop(1, planes, lambda k: sides(k, project_plane))
    turn = jnp.where(2 * plane < planes, planes - 1, 1)

    def tally_plane(j):
        p = lax.rem(plane + turn * j, planes)
        loop(0, ROWS, lambda r: tally_chip(p, lax.rem(row + r, ROWS)))

    loop(0, planes, tally_plane)
    f_buf[me] = acc[0:queries, :]
    others(lambda t: small_copy(f_buf, f_send, f_recv, me, t).start())

    def left(slot, channel):
        for part in range(PARTS):
            x_copy(x_all.at[slot], slot, channel, across, part).wait_send()

    def drain(p):
        slot = slot_of(p, row, core)

        @pl.when((p <= plane) & has_up)
        def _():
            left(slot, 0)

        @pl.when((p >= plane) & has_down)
        def _():
            left(slot, 1)

        left(slot, 2)
        left(slot, 3)
        left(slot_of(p, 1 - row, core), 3)

    loop(0, planes, drain)
    all_sent(y_all, y_send)
    all_sent(e_buf, e_send)
    all_sent(f_buf, f_recv)
    all_sent(f_buf, f_send)
    summed = jnp.sum(f_buf[...], axis=0)
    lane = lax.broadcasted_iota(jnp.int32, summed.shape, 1)
    per_device = out_ref.shape[0]
    for j in range(per_device):
        picked = jnp.sum(jnp.where(lane == me * per_device + j, summed, 0.0), axis=1, keepdims=True)
        for q in range(queries):
            out_ref[j:j + 1, q:q + 1] = picked[q:q + 1, :]


def fused(n, layer_inputs, output_grads, query_grads, eigenvalues, out_basis, in_basis, doc_lengths):
    tokens, width_in = layer_inputs.shape
    tiles, queries, rows_out, rows_in = query_grads.shape
    docs = doc_lengths.shape[0]
    block = out_basis.shape[1]
    anyspace = pl.BlockSpec(memory_space=pl.ANY)
    vmem = pl.BlockSpec(memory_space=pltpu.VMEM)
    bf16, f32 = jnp.bfloat16, jnp.float32
    return pl.pallas_call(
        functools.partial(fused_kernel, n, output_grads.shape[1] * width_in),
        out_shape=jax.ShapeDtypeStruct((docs // n, queries), f32),
        in_specs=[anyspace] * 6 + [vmem],
        out_specs=vmem,
        scratch_shapes=[
            pltpu.VMEM((n, tokens, width_in), bf16),
            pltpu.VMEM((n, tokens, rows_out), bf16),
            pltpu.VMEM(query_grads.shape, bf16),
            pltpu.VMEM(eigenvalues.shape, f32),
            pltpu.VMEM((rows_out // block, block, block), bf16),
            pltpu.VMEM(in_basis.shape, bf16),
            pltpu.VMEM((rows_out // block, block, block), bf16),
            pltpu.VMEM((queries * rows_out, width_in), bf16),
            pltpu.VMEM((CORES * tokens, width_in), bf16),
            pltpu.VMEM((CORES * tokens, rows_out), f32),
            pltpu.VMEM((n // CORES, CORES * tokens, queries * rows_out), f32),
            pltpu.VMEM((8, LANES), f32),
            pltpu.VMEM((n, 1, LANES), f32),
            pltpu.VMEM((n, queries, LANES), f32),
            pltpu.VMEM((8, LANES), f32),
            pltpu.SemaphoreType.DMA((6,)),
            pltpu.SemaphoreType.DMA((n * PARTS, 4)),
            pltpu.SemaphoreType.DMA((n * PARTS,)),
            pltpu.SemaphoreType.DMA,
            pltpu.SemaphoreType.DMA((n,)),
        ] + [pltpu.SemaphoreType.DMA] * 4 + [pltpu.SemaphoreType.REGULAR] * 3,
        compiler_params=pltpu.CompilerParams(
            collective_id=0, has_side_effects=True, vmem_limit_bytes=55040 * 1024
        ),
    )(layer_inputs, output_grads, query_grads, eigenvalues, out_basis, in_basis, doc_lengths[None])


def local(n, *arrays):
    layer_inputs, output_grads, query_grads, _, _, _, doc_lengths = arrays
    tiles, queries, rows_out, rows_in = query_grads.shape
    whole_rows = tiles * rows_in == layer_inputs.shape[1] and n * rows_out == output_grads.shape[1]
    fits = n * layer_inputs.size <= 8 * query_grads.size and doc_lengths.shape[0] <= LANES
    shaped = n % (CORES * ROWS) == 0 and doc_lengths.shape[0] % n == 0 and queries <= 8
    shaped = shaped and layer_inputs.shape[0] % (16 * PARTS) == 0 and n > CORES * ROWS
    if whole_rows and fits and shaped:
        return fused(n, *arrays)
    return tiles_apart(*arrays)


def solution(mesh):
    in_specs = (
        P(("groups", "dp"), None),
        P(("groups", "dp"), None),
        P("dp", None, None, None),
        P("dp", None, None),
        P(),
        P(),
        P("groups"),
    )
    out_specs = P(("groups", "dp"), None)
    return jax.shard_map(functools.partial(local, mesh.shape["dp"]), mesh=mesh, in_specs=in_specs, out_specs=out_specs, check_vma=False)
```
